256 devices in a mesh: dp: 8 (over y, core), expert: 32 (over z, x).
Axes of the slice: x: 4, y: 4, z: 8, core: 2. Of those that a mesh axis runs over, the one named last changes fastest.
Arguments:
- tokens: bfloat16 [4096, 7168], P('expert', 'dp'), may hold values from -6 to 6
- cotangent: bfloat16 [4096, 7168], P('expert', 'dp'), may hold values from -6 to 6
- expert_ids: int32 [4096, 8], P('expert'), may hold values from 0 to 31, all different within a row; in each aligned block of 128 rows (0 to 127, 128 to 255, ...) at most 40 rows name the same one
- gates: float32 [4096, 8], P('expert'), may hold values from 0.05 to 0.5
- up_weight: bfloat16 [32, 7168, 1024], P('expert', 'dp'), may hold values from -0.0625 to 0.0625
- down_weight: bfloat16 [32, 1024, 7168], P('expert', None, 'dp'), may hold values from -0.1875 to 0.1875
Outputs:
- mixed: bfloat16 [4096, 7168], P('expert', 'dp')
- input_grads: bfloat16 [4096, 7168], P('expert', 'dp')
- up_grads: bfloat16 [32, 7168, 1024], P('expert', 'dp')
- down_grads: bfloat16 [32, 1024, 7168], P('expert', None, 'dp')
- gate_grads: float32 [4096, 8], P('expert')
The draws below stay inside these ranges and needn't reach their ends.
Inputs may be any that keep to these rules, and one draw needn't show every extreme that they name: `expert_ids`: each row names 8 different experts. In the rows of one index of the expert axis no expert is named by more than 40 rows, a bound that some block reaches of them.
All inputs are finite; a program needn't handle non-finite values.
Results may differ from the reference program's by a relative error of at most 0.0064.
Values may be sent and summed in bfloat16 or wider, within the bound.
No kernel may reach another device: no remote copies, remote signals or barrier semaphores. Data moves between devices by JAX's collectives and lax.ppermute only.
A program may use at most 128 MiB of HBM per device.

```python
import math
import jax
import jax.numpy as jnp
import numpy as np
from jax import lax

D = 7168
FF = 1024
TOPK = 8
TOK_DEV = 128
EXPERTS = 32
CAP = 40
SLOTS = 1280
TOKENS = 4096


def block_scale(own_key, shape, split, smallest, top_value):
    gain, own = 1.0, jax.random.fold_in(own_key, 6)
    for dim, shards_of in split:
        heights = jnp.exp(jax.random.uniform(jax.random.fold_in(own, dim), (shards_of,), jnp.float32, smallest / len(split), top_value / len(split)))
        gain = gain * jnp.repeat(heights, shape[dim] // shards_of).reshape([-1 if axis == dim else 1 for axis in range(len(shape))])
    return gain


def routed_block(rng, own, number, rows, count, top, limit, slope):
    sequence = jax.random.permutation(rng, count)
    packed, usual = load_shares(count, rows * top, limit, slope, True), load_shares(count, rows * top, limit, slope, False)
    places = jnp.arange(count)

    def named(tallies, turn):
        used = int((tallies > 0).sum())
        fixed = max(1, used // 4)
        moved = fixed + (places - fixed + turn * (used - fixed)) % max(1, count - fixed)
        return jnp.zeros((count,), jnp.int32).at[sequence[jnp.where(places < fixed, places, moved)]].set(jnp.asarray(tallies, jnp.int32))

    tallies = jnp.where(number % 4 == 0, named(packed, number // 4), named(usual, number - number // 4 - 1))
    mixed = jax.random.permutation(jax.random.fold_in(own, 3), count)
    donor, sink = mixed[0:count // 2 * 2:2], mixed[1:count // 2 * 2:2]
    margin = jnp.minimum(tallies[donor] - 1, limit - tallies[sink]) // 2
    margin = jnp.where((donor == sequence[0]) | (sink == sequence[0]) | (tallies[sink] == 0), 0, jnp.maximum(margin, 0))
    moved = jax.random.randint(jax.random.fold_in(own, 4), (count // 2,), 0, 1 << 20) % (margin + 1)
    tallies = tallies.at[donor].add(-moved).at[sink].add(moved)
    members = jnp.searchsorted(jnp.cumsum(tallies), jnp.arange(rows * top), side="right").astype(jnp.int32)
    grid = members.reshape(top, rows).T
    grid = grid[jax.random.permutation(jax.random.fold_in(own, 1), rows)]
    turn = jax.random.randint(jax.random.fold_in(own, 2), (rows, 1), 0, top)
    return jnp.take_along_axis(grid, (jnp.arange(top)[None, :] + turn) % top, axis=1)


def load_shares(amount, total, reach, lean, full):
    portions = [(1 << 20) // math.isqrt(grade ** lean) + 1 for grade in range(1, amount + 1)]
    largest = reach if full else min(reach, max(-(-total // amount), total * portions[0] // sum(portions)))
    least = 1 if total - largest >= amount - 1 else 0
    given, spare = [largest] + [least] * (amount - 1), total - largest - least * (amount - 1)
    while spare > 0:
        movable = [i for i in range(1, amount) if given[i] < largest] or [i for i in range(1, amount) if given[i] < reach]
        whole, left = sum([portions[i] for i in movable]), spare
        for i in movable:
            extra = min(reach - given[i], max(1, left * portions[i] // whole), spare)
            given[i] = given[i] + extra
            spare = spare - extra
    return np.array(given)


def normal_values(rng, extent, deviation, reach, split=(), kind=jnp.bfloat16):
    drawn = deviation * jax.random.normal(rng, extent, jnp.float32)
    if split:
        drawn = drawn * block_scale(rng, extent, split, -0.22, 0.18)
    return jnp.clip(drawn, -reach, reach).astype(kind)


def setup_inputs(seed: int = 0) -> dict:
    arg_keys = jax.random.split(jax.random.key(seed), 7)
    tokens = normal_values(arg_keys[0], (TOKENS, D), 1.0, 6.0, ((0, 32), (1, 8)))
    cotangent = normal_values(arg_keys[1], (TOKENS, D), 1.0, 6.0, ((0, 32), (1, 8)))
    expert_ids_keys = jax.random.split(jax.random.fold_in(arg_keys[2], 1), TOKENS // TOK_DEV)
    expert_ids_turns = jax.random.permutation(jax.random.fold_in(arg_keys[2], 3), TOKENS // TOK_DEV)
    expert_ids = jax.vmap(lambda own, number: routed_block(jax.random.fold_in(arg_keys[2], 2), own, number, TOK_DEV, EXPERTS, TOPK, CAP, 2))(expert_ids_keys, expert_ids_turns).reshape((TOKENS, TOPK))
    gates = jnp.clip(jnp.exp(math.log(0.5) - 2.3025851 * jax.random.uniform(arg_keys[3], (TOKENS, TOPK), jnp.float32) ** block_scale(arg_keys[3], (TOKENS, TOPK), ((0, 32),), -0.2, 0.2)), 0.05, 0.5)
    up_weight = normal_values(arg_keys[4], (EXPERTS, D, FF), D ** -0.5, 0.0625, ((0, 32), (1, 8)))
    down_weight = normal_values(arg_keys[5], (EXPERTS, FF, D), FF ** -0.5, 0.1875, ((0, 32), (2, 8)))
    return dict(tokens=tokens, cotangent=cotangent, expert_ids=expert_ids, gates=gates, up_weight=up_weight, down_weight=down_weight)


def silu_slope(preact):
    logistic = jax.nn.sigmoid(preact)
    return logistic * (1.0 + preact * (1.0 - logistic))


def reference(tokens, cotangent, expert_ids, gates, up_weight, down_weight):
    assigned = expert_ids.reshape(EXPERTS, TOK_DEV * TOPK)
    labels = jnp.arange(EXPERTS, dtype=jnp.int32)
    chosen = (assigned[:, :, None] == labels[None, None, :]).astype(jnp.int32)
    before = jnp.cumsum(chosen, axis=1) - chosen
    position = jnp.sum(before * chosen, axis=2)
    source = jnp.arange(EXPERTS, dtype=jnp.int32)[:, None]
    slot_rows = (source * CAP + position).reshape(-1).astype(jnp.int32)
    target = (assigned.reshape(-1) * SLOTS + slot_rows).astype(jnp.int32)
    filled = jnp.full((EXPERTS * SLOTS,), -1, jnp.int32)
    filled = filled.at[target].set(jnp.arange(TOKENS * TOPK, dtype=jnp.int32))
    filled = filled.reshape(EXPERTS, SLOTS)
    flat_gates = gates.reshape(-1)

    def one_expert(operands):
        owner_rows, w_up, w_down = operands
        valid = owner_rows >= 0
        safe_rows = jnp.maximum(owner_rows, 0).astype(jnp.int32)
        token_rows = (safe_rows // TOPK).astype(jnp.int32)
        x_slots = jnp.where(valid[:, None], tokens[token_rows], jnp.zeros((), tokens.dtype))
        scaled = (flat_gates[safe_rows][:, None] * cotangent[token_rows].astype(jnp.float32)).astype(jnp.bfloat16)
        g_slots = jnp.where(valid[:, None], scaled, jnp.zeros((), scaled.dtype))
        preact = jnp.dot(x_slots, w_up, preferred_element_type=jnp.float32)
        hidden = jax.nn.silu(preact).astype(jnp.bfloat16)
        outputs = jnp.dot(hidden, w_down, preferred_element_type=jnp.float32).astype(jnp.bfloat16)
        hidden_grad = jnp.dot(g_slots, w_down.T, preferred_element_type=jnp.float32)
        preact_grad = (hidden_grad * silu_slope(preact)).astype(jnp.bfloat16)
        slot_dx = jnp.dot(preact_grad, w_up.T, preferred_element_type=jnp.float32).astype(jnp.bfloat16)
        down_grad = jnp.dot(hidden.T, g_slots, preferred_element_type=jnp.float32).astype(jnp.bfloat16)
        up_grad = jnp.dot(x_slots.T, preact_grad, preferred_element_type=jnp.float32).astype(jnp.bfloat16)
        return outputs, slot_dx, up_grad, down_grad

    out_slots, dx_slots, up_grads, down_grads = lax.map(one_expert, (filled, up_weight, down_weight))
    expert_out = out_slots.reshape(EXPERTS * SLOTS, D)[target].reshape(TOKENS, TOPK, D).astype(jnp.float32)
    mixed = jnp.sum(gates[:, :, None] * expert_out, axis=1).astype(jnp.bfloat16)
    gate_grads = jnp.sum(cotangent[:, None, :].astype(jnp.float32) * expert_out, axis=2)
    back_dx = dx_slots.reshape(EXPERTS * SLOTS, D)[target].reshape(TOKENS, TOPK, D).astype(jnp.float32)
    input_grads = jnp.sum(back_dx, axis=1).astype(jnp.bfloat16)
    return mixed, input_grads, up_grads, down_grads, gate_grads
```

```python
import jax
import jax.numpy as jnp
from jax import lax
from jax.experimental import pallas as pl
from jax.experimental.pallas import tpu as pltpu
from jax.sharding import Mesh
from jax.sharding import PartitionSpec as P

BF = jnp.bfloat16
F32 = jnp.float32

NZ, NX, NY = 8, 4, 4


def shift(value, axis, size, by):
    return lax.ppermute(value, axis, [(i, (i + by) % size) for i in range(size)])


def ring_gather_z(block, half):
    blocks = [None] * NZ
    blocks[0] = block
    up, down = block, block
    for step in range(1, NZ // 2):
        up = shift(up, "z", NZ, 1)
        down = shift(down, "z", NZ, -1)
        blocks[NZ - step], blocks[step] = up, down
    first = shift(up[:half], "z", NZ, 1)
    second = shift(down[half:], "z", NZ, -1)
    blocks[NZ // 2] = jnp.concatenate([first, second], axis=0)
    return blocks


def ring_sum_z(parts):
    tok = parts[0].shape[0]
    half = tok // 2
    far = parts[NZ // 2]
    up = shift(far[:half], "z", NZ, 1)
    down = shift(far[half:], "z", NZ, -1)
    for step in range(NZ // 2 - 1, 0, -1):
        a, b = parts[step].astype(F32), parts[NZ - step].astype(F32)
        if step == NZ // 2 - 1:
            a = jnp.concatenate([a[:half] + up.astype(F32), a[half:]], axis=0)
            b = jnp.concatenate([b[:half], b[half:] + down.astype(F32)], axis=0)
        else:
            a, b = a + up.astype(F32), b + down.astype(F32)
        up = shift(a.astype(BF), "z", NZ, 1)
        down = shift(b.astype(BF), "z", NZ, -1)
    return (parts[0].astype(F32) + up.astype(F32) + down.astype(F32)).astype(BF)


def exchange(blocks, axis, size):
    half = blocks[2].shape[0] // 2
    far_up = shift(blocks[2][:half], axis, size, 1)
    far_down = shift(blocks[2][half:], axis, size, -1)
    from_before = shift(blocks[1], axis, size, 1)
    from_after = shift(blocks[3], axis, size, -1)
    far_up = shift(far_up, axis, size, 1)
    far_down = shift(far_down, axis, size, -1)
    return [blocks[0], from_after, jnp.concatenate([far_up, far_down], axis=0), from_before]


def ring_gather_y(block):
    half = block.shape[0] // 2
    before = shift(block, "y", NY, 1)
    after = shift(block, "y", NY, -1)
    first = shift(before[:half], "y", NY, 1)
    second = shift(after[half:], "y", NY, -1)
    return [block, after, jnp.concatenate([first, second], axis=0), before]


def select_kernel(scaled, pick_ref, gate_ref, *refs):
    blocks, outs = refs[:NZ], refs[NZ:]
    tok = 128
    cap = outs[0].shape[2]
    for p in range(NZ // 2):
        pair = jnp.concatenate([blocks[p][:tok, :], blocks[p + NZ // 2][:tok, :]], axis=0)
        pick = pick_ref[p]
        rows = jnp.dot(pick, pair, preferred_element_type=F32)
        if scaled:
            weight = jnp.sum(pick.astype(F32) * gate_ref[p], axis=1, keepdims=True)
            rows = rows * weight
        rows = rows.astype(BF)
        for dx in range(NX):
            for h in range(2):
                at = (dx * 2 + h) * cap
                outs[dx][h, p] = rows[at : at + cap]


def select_rows(pick, gate_rows, blocks, scaled, cap):
    width = blocks[0].shape[1]
    outs = pl.pallas_call(
        lambda *refs: select_kernel(scaled, *refs),
        out_shape=[jax.ShapeDtypeStruct((2, NZ // 2, cap, width), BF)] * NX,
        name="select_scaled" if scaled else "select_plain",
    )(pick, gate_rows, *blocks)
    return [o.reshape(2 * (NZ // 2) * cap, width) for o in outs]


def mix_kernel(pieces, tok, *refs):
    picks, rows, outs = refs[:pieces], refs[pieces : pieces + NX], refs[pieces + NX :]
    for p in range(NZ // 2):
        stack = jnp.concatenate(
            [rows[dx][h, p] for dx in range(NX) for h in range(2)], axis=0
        )
        total = None
        for ref in picks:
            part = lax.dot_general(
                ref[p], stack, (((0,), (0,)), ((), ())), preferred_element_type=F32
            )
            total = part if total is None else total + part
        total = total.astype(BF)
        outs[p][...] = total[:tok]
        outs[p + NZ // 2][...] = total[tok:]


def mix_rows(picks, rows, tok, cap):
    width = rows[0].shape[1]
    rows = [r.reshape(2, NZ // 2, cap, width) for r in rows]
    return pl.pallas_call(
        lambda *refs: mix_kernel(len(picks), tok, *refs),
        out_shape=[jax.ShapeDtypeStruct((tok, width), BF)] * NZ,
        name="mix%d" % len(picks),
    )(*picks, *rows)


def ranks_before(chosen):
    count = chosen.shape[-1]
    earlier = lax.broadcasted_iota(jnp.int32, (count, count), 0)
    later = lax.broadcasted_iota(jnp.int32, (count, count), 1)
    strict = (earlier < later).astype(BF)
    return jnp.dot(chosen.astype(BF), strict, preferred_element_type=F32)


def split3(value):
    hi = lax.reduce_precision(value, 8, 7)
    mid = lax.reduce_precision(value - hi, 8, 7)
    low = value - hi - mid
    return hi.astype(BF), mid.astype(BF), low.astype(BF)


def per_device(tokens, cotangent, expert_ids, gates, up_weight, down_weight):
    tok, width = tokens.shape
    top = expert_ids.shape[1]
    experts = NZ * NX
    cap = tok * top * 5 // (4 * experts)
    slots = experts * cap
    block = slots // NX
    y, core = lax.axis_index("y"), lax.axis_index("core")
    z, x = lax.axis_index("z"), lax.axis_index("x")
    w_up, w_down = up_weight[0], down_weight[0]
    hid = w_up.shape[1]

    ids_t, gates_t = expert_ids.T, gates.T
    meta = jnp.concatenate(
        [ids_t.astype(BF), *split3(gates_t), jnp.zeros((top, width - 4 * tok), BF)], axis=1
    )
    x_blocks = ring_gather_z(jnp.concatenate([tokens, meta], axis=0), 72)
    c_blocks = ring_gather_z(cotangent, 64)

    meta = jnp.stack([b[tok:, : 4 * tok] for b in x_blocks])
    ids_d = meta[:, :, :tok].astype(F32)
    gates_d = sum(meta[:, :, i * tok : (i + 1) * tok].astype(F32) for i in (1, 2, 3))
    labels = (z * NX + (x + jnp.arange(NX)) % NX).astype(F32)
    hit = ids_d[:, None] == labels[None, :, None, None]
    gate_of = jnp.sum(jnp.where(hit, gates_d[:, None], 0.0), axis=2)
    hit = hit.any(axis=2)
    rank = ranks_before(hit.reshape(NZ * NX, tok)).reshape(NZ, NX, tok)
    place = jnp.where(hit, rank, -1.0)
    pair = NZ // 2
    low, high = place[:pair], place[pair:]
    nothing = jnp.full_like(low, -1.0)
    zero_core = core == 0
    mine = jnp.concatenate(
        [jnp.where(zero_core, low, nothing), jnp.where(zero_core, nothing, high)], axis=2
    )
    other = jnp.concatenate(
        [jnp.where(zero_core, nothing, low), jnp.where(zero_core, high, nothing)], axis=2
    )
    both = jnp.stack([mine, other], axis=2)
    pick = both[:, :, :, None, :] == jnp.arange(cap, dtype=F32)[None, None, None, :, None]
    gate_pair = jnp.concatenate([gate_of[:pair], gate_of[pair:]], axis=2)
    gate_rows = jnp.broadcast_to(gate_pair[:, :, None, None, :], pick.shape)
    gate_rows = jnp.where(pick, gate_rows, 0.0).reshape(pair, NX * 2 * cap, 2 * tok)
    pick = pick.astype(BF).reshape(pair, NX * 2 * cap, 2 * tok)
    gate_hi = lax.reduce_precision(gate_rows, 8, 7)
    gate_lo = (gate_rows - gate_hi).astype(BF)
    gate_hi = gate_hi.astype(BF)

    x_recv = exchange(select_rows(pick, gate_rows, x_blocks, False, cap), "x", NX)
    c_recv = exchange(select_rows(pick, gate_rows, c_blocks, True, cap), "x", NX)
    x_slots = jnp.concatenate(x_recv, axis=0)
    g_slots = jnp.concatenate(c_recv, axis=0)

    def reduce(slot_rows, weight, contract):
        rows = slot_rows.reshape(NX, 2, block // 2, width)
        dims = (((2,), (contract,)), ((), ()))
        away = lax.dot_general(rows[:, 1], weight, dims, preferred_element_type=F32).astype(BF)
        keep = lax.dot_general(rows[:, 0], weight, dims, preferred_element_type=F32)
        keep = keep + shift(away, "core", 2, 1).astype(F32)
        parts = [
            lax.dynamic_index_in_dim(keep, (y + dy) % NY, 0, keepdims=False) for dy in range(NY)
        ]
        got = exchange([parts[0]] + [p.astype(BF) for p in parts[1:]], "y", NY)
        return sum(g.astype(F32) for g in got)

    def spread(part):
        ring = jnp.stack(ring_gather_y(part))
        ring = jnp.stack([ring, shift(ring, "core", 2, 1)], axis=1)
        return [
            lax.dynamic_index_in_dim(ring, (dx - y) % NY, 0, keepdims=False).reshape(block, hid)
            for dx in range(NX)
        ]

    pre = reduce(x_slots, w_up, 0)
    logistic = jax.nn.sigmoid(pre)
    hidden_part = pre * logistic
    hidden = spread(hidden_part.astype(BF))
    out_rows = [
        jnp.dot(h, w_down, preferred_element_type=F32).astype(BF) for h in hidden
    ]
    mixed = ring_sum_z(mix_rows((gate_hi, gate_lo), exchange(out_rows, "x", NX), tok, cap))

    raw = reduce(g_slots, w_down, 1)
    slot_gg = jnp.sum(hidden_part * raw, axis=1)
    pre_grad = spread((raw * (logistic * (1.0 + pre * (1.0 - logistic)))).astype(BF))
    dx_rows = [
        lax.dot_general(g, w_up, (((1,), (1,)), ((), ())), preferred_element_type=F32).astype(BF)
        for g in pre_grad
    ]
    input_grads = ring_sum_z(mix_rows((pick,), exchange(dx_rows, "x", NX), tok, cap))

    down_grad = lax.dot_general(
        jnp.concatenate(hidden, axis=0), g_slots, (((0,), (0,)), ((), ())),
        preferred_element_type=F32,
    ).astype(BF)
    up_grad = lax.dot_general(
        x_slots, jnp.concatenate(pre_grad, axis=0), (((0,), (0,)), ((), ())),
        preferred_element_type=F32,
    ).astype(BF)

    ring = jnp.stack(
        [slot_gg] + [shift(slot_gg, "y", NY, -dy) for dy in range(1, NY)]
    )
    away = shift(ring, "core", 2, 1)
    ring = jnp.stack([jnp.where(zero_core, ring, away), jnp.where(zero_core, away, ring)], axis=1)
    by_dx = jnp.roll(ring, y, axis=0).reshape(NX, NZ, cap)
    by_group = jnp.roll(jnp.roll(by_dx, x, axis=0), z, axis=1)
    gg = by_group.transpose(1, 0, 2).reshape(experts, cap)
    gg = lax.all_to_all(gg, ("z", "x"), split_axis=0, concat_axis=0, tiled=True)
    own = ids_t[:, None, :] == jnp.arange(experts, dtype=jnp.int32)[None, :, None]
    token_hit = own.any(axis=0)
    token_place = jnp.where(token_hit, ranks_before(token_hit), -1.0)
    at = token_place[:, None, :] == jnp.arange(cap, dtype=F32)[None, :, None]
    value = jnp.sum(jnp.where(at, gg[:, :, None], 0.0), axis=1)
    gate_grads = (jnp.sum(jnp.where(own, value[None], 0.0), axis=1) / gates_t).T
    return mixed, input_grads, up_grad[None], down_grad[None], gate_grads


def solution(mesh):
    grid = Mesh(mesh.devices.reshape(NY, 2, NZ, NX), ("y", "core", "z", "x"))
    dp, ex = ("y", "core"), ("z", "x")
    return jax.shard_map(
        per_device,
        mesh=grid,
        in_specs=(P(ex, dp), P(ex, dp), P(ex, None), P(ex, None), P(ex, dp, None), P(ex, None, dp)),
        out_specs=(P(ex, dp), P(ex, dp), P(ex, dp, None), P(ex, None, dp), P(ex, None)),
        check_vma=False,
    )
```

```python
import jax
import jax.numpy as jnp
from jax import lax
from jax.experimental import pallas as pl
from jax.experimental.pallas import tpu as pltpu
from jax.sharding import Mesh
from jax.sharding import PartitionSpec as P

BF = jnp.bfloat16
F32 = jnp.float32

NZ, NX, NY = 8, 4, 4
PAIRS = NZ // 2
MEMBERS = (0, 1, -1, -2, 2, 3, -3, -4)


ANY = pl.BlockSpec(memory_space=pl.ANY)
VMEM = pl.BlockSpec(memory_space=pltpu.VMEM)
SMEM = pl.BlockSpec(memory_space=pltpu.SMEM)


def swap(value, axis, size, turn):
    pairs = []
    for c in range(2):
        for i in range(size):
            side = 1 if (i + c + turn) % 2 == 0 else -1
            to = (i + side) % size
            pairs.append((2 * i + c, 2 * to + c) if axis == "y" else (c * size + i, c * size + to))
    return lax.ppermute(value, ("y", "core") if axis == "y" else ("core", axis), pairs)


def swap_core(value):
    return lax.ppermute(value, "core", [(0, 1), (1, 0)])


def tie(value, *others):
    return lax.optimization_barrier((value, *others))[0]


def gather_z(block, join):
    first = swap(block, "z", NZ, 0)
    pairs = [join(block, first)]
    for turn in (1, 0, 1):
        pairs.append(swap(pairs[-1], "z", NZ, turn))
    return pairs


def sum_z(parts):
    tok = parts[0].shape[0] // 2
    total = parts[3]
    for k, turn in ((2, 1), (1, 0), (0, 1)):
        got = swap(total, "z", NZ, turn)
        if k:
            total = (parts[k].astype(F32) + got.astype(F32)).astype(BF)
    last = (parts[0][tok:].astype(F32) + got[tok:].astype(F32)).astype(BF)
    end = swap(last, "z", NZ, 0)
    return (parts[0][:tok].astype(F32) + got[:tok].astype(F32) + end.astype(F32)).astype(BF)


def exchange(blocks):
    own, first, second, opposite = blocks
    far = swap(opposite, "x", NX, 0)
    from_first = swap(first, "x", NX, 0)
    from_second = swap(second, "x", NX, 1)
    from_opposite = swap(far, "x", NX, 1)
    return [own, from_first, from_second, from_opposite]


def select_rows(table, pick, weights, pairs, cap):
    tok2, width = pick.shape[2], pairs[0].shape[1]
    scaled = bool(weights)

    def kernel(table_ref, pick_ref, *refs):
        weight_refs, refs = refs[: len(weights)], refs[len(weights) :]
        blocks, outs, (held, sems) = refs[:PAIRS], refs[PAIRS : PAIRS + NX], refs[PAIRS + NX :]
        copies = [
            pltpu.make_async_copy(blocks[k].at[pl.ds(0, tok2)], held.at[k], sems.at[k])
            for k in range(PAIRS)
        ]
        for c in copies:
            c.start()
        for c in copies:
            c.wait()

        def step(k, carry):
            rows = jnp.dot(pick_ref[k], held[k], preferred_element_type=F32)
            if scaled:
                weight = sum(
                    jnp.sum(w[k].astype(F32), axis=1, keepdims=True) for w in weight_refs
                )
                rows = rows * weight
            rows = rows.astype(BF)
            for i in range(NX):
                for j in range(2):
                    at = (i * 2 + j) * cap
                    outs[i][table_ref[2 * k + j]] = rows[at : at + cap]
            return carry

        lax.fori_loop(0, PAIRS, step, 0)

    outs = pl.pallas_call(
        kernel,
        out_shape=[jax.ShapeDtypeStruct((NZ, cap, width), BF)] * NX,
        in_specs=[SMEM, VMEM] + [VMEM] * len(weights) + [ANY] * PAIRS,
        out_specs=[VMEM] * NX,
        scratch_shapes=[pltpu.VMEM((PAIRS, tok2, width), BF), pltpu.SemaphoreType.DMA((PAIRS,))],
        cost_estimate=pl.CostEstimate(flops=600_000_000, bytes_accessed=5_000_000, transcendentals=0),
        name="select_scaled" if scaled else "select_plain",
    )(table, pick, *weights, *pairs)
    return [o.reshape(NZ * cap, width) for o in outs]


def mix_rows(table, picks, rows, cap):
    tok2, width = picks[0].shape[2], rows[0].shape[1]
    rows = [r.reshape(NZ, cap, width) for r in rows]

    def kernel(table_ref, *refs):
        pick_refs, refs = refs[: len(picks)], refs[len(picks) :]
        blocks, outs, (held, made, sems, out_sems) = refs[:NX], refs[NX : NX + PAIRS], refs[NX + PAIRS :]
        copies = [pltpu.make_async_copy(blocks[i], held.at[i], sems.at[i]) for i in range(NX)]
        for c in copies:
            c.start()
        for c in copies:
            c.wait()
        puts = [pltpu.make_async_copy(made.at[k], outs[k], out_sems.at[k]) for k in range(PAIRS)]

        def step(n, carry):
            k = PAIRS - 1 - n
            stack = jnp.concatenate(
                [held[i, table_ref[2 * k + j]] for i in range(NX) for j in range(2)], axis=0
            )
            total = None
            for ref in pick_refs:
                part = lax.dot_general(
                    ref[k], stack, (((0,), (0,)), ((), ())), preferred_element_type=F32
                )
                total = part if total is None else total + part
            made[k] = total.astype(BF)
            for m in range(PAIRS):
                pl.when(k == m)(puts[m].start)
            return carry

        lax.fori_loop(0, PAIRS, step, 0)
        for put in puts:
            put.wait()

    return pl.pallas_call(
        kernel,
        out_shape=[jax.ShapeDtypeStruct((tok2, width), BF)] * PAIRS,
        in_specs=[SMEM] + [VMEM] * len(picks) + [ANY] * NX,
        out_specs=[ANY] * PAIRS,
        scratch_shapes=[
            pltpu.VMEM((NX, NZ, cap, width), BF),
            pltpu.VMEM((PAIRS, tok2, width), BF),
            pltpu.SemaphoreType.DMA((NX,)),
            pltpu.SemaphoreType.DMA((PAIRS,)),
        ],
        cost_estimate=pl.CostEstimate(flops=600_000_000 * len(picks), bytes_accessed=5_000_000, transcendentals=0),
        name="mix%d" % len(picks),
    )(table, *picks, *rows)


def partial_sums(table, offset, half, blocks, weight, contract, dtype):
    rows, width = blocks[0].shape[0] // 2, blocks[0].shape[1]
    hid = weight.shape[1 - contract]

    def kernel(table_ref, weight_ref, *refs):
        ins, (out, held, sems) = refs[:NX], refs[NX:]
        copies = [
            pltpu.make_async_copy(ins[i].at[pl.ds(half * rows, rows)], held.at[i], sems.at[i])
            for i in range(NX)
        ]
        for c in copies:
            c.start()
        for c in copies:
            c.wait()

        def step(i, carry):
            out[table_ref[offset + i]] = lax.dot_general(
                held[i], weight_ref[...], (((1,), (contract,)), ((), ())),
                preferred_element_type=F32,
            ).astype(dtype)
            return carry

        lax.fori_loop(0, NX, step, 0)

    return pl.pallas_call(
        kernel,
        out_shape=jax.ShapeDtypeStruct((NX, rows, hid), dtype),
        in_specs=[SMEM, VMEM] + [ANY] * NX,
        out_specs=VMEM,
        scratch_shapes=[pltpu.VMEM((NX, rows, width), BF), pltpu.SemaphoreType.DMA((NX,))],
        cost_estimate=pl.CostEstimate(flops=1_200_000_000, bytes_accessed=6_000_000, transcendentals=0),
        name="partial%d%d" % (half, contract),
    )(table, weight, *blocks)


def expand_rows(table, offset, shares, weight, contract):
    rows, hid = shares[0].shape[1], shares[0].shape[2]
    width = weight.shape[1 - contract]

    def kernel(table_ref, weight_ref, *refs):
        ins, refs = refs[:4], refs[4:]
        outs, joined, (held, made, in_sems, out_sems, join_sems) = refs[:NX], refs[NX], refs[NX + 1 :]
        copies = [
            pltpu.make_async_copy(ins[n], held.at[n // 2, pl.ds((n % 2) * 2, 2)], in_sems.at[n])
            for n in range(4)
        ]
        for c in copies:
            c.start()
        for c in copies:
            c.wait()
        puts = [pltpu.make_async_copy(made.at[i], outs[i], out_sems.at[i]) for i in range(NX)]

        def keep(i, h):
            return pltpu.make_async_copy(
                held.at[h, table_ref[offset + NX * h + i]], joined.at[i, h], join_sems.at[i, h]
            )

        def step(n, carry):
            i = NX - 1 - n
            for h in range(2):
                keep(i, h).start()
                made[i, h] = lax.dot_general(
                    held[h, table_ref[offset + NX * h + i]], weight_ref[...],
                    (((1,), (contract,)), ((), ())), preferred_element_type=F32,
                ).astype(BF)
            for m in range(NX):
                pl.when(i == m)(puts[m].start)
            return carry

        lax.fori_loop(0, NX, step, 0)
        for put in puts:
            put.wait()
        for i in range(NX):
            for h in range(2):
                keep(i, h).wait()

    *outs, joined = pl.pallas_call(
        kernel,
        out_shape=[jax.ShapeDtypeStruct((2, rows, width), BF)] * NX
        + [jax.ShapeDtypeStruct((NX, 2, rows, hid), BF)],
        in_specs=[SMEM, VMEM] + [ANY] * 4,
        out_specs=[ANY] * (NX + 1),
        scratch_shapes=[
            pltpu.VMEM((2, NY, rows, hid), BF),
            pltpu.VMEM((NX, 2, rows, width), BF),
            pltpu.SemaphoreType.DMA((4,)),
            pltpu.SemaphoreType.DMA((NX,)),
            pltpu.SemaphoreType.DMA((NX, 2)),
        ],
        cost_estimate=pl.CostEstimate(flops=2_400_000_000, bytes_accessed=9_000_000, transcendentals=0),
        name="expand%d" % contract,
    )(table, weight, *shares)
    return [o.reshape(2 * rows, width) for o in outs], joined.reshape(NX * 2 * rows, hid)


def ranks_before(chosen):
    count = chosen.shape[-1]
    earlier = lax.broadcasted_iota(jnp.int32, (count, count), 0)
    later = lax.broadcasted_iota(jnp.int32, (count, count), 1)
    strict = (earlier < later).astype(BF)
    return jnp.dot(chosen.astype(BF), strict, preferred_element_type=F32)


def split3(value):
    hi = lax.reduce_precision(value, 8, 7)
    mid = lax.reduce_precision(value - hi, 8, 7)
    low = value - hi - mid
    return hi.astype(BF), mid.astype(BF), low.astype(BF)


def per_device(tokens, cotangent, expert_ids, gates, up_weight, down_weight):
    tok, width = tokens.shape
    top = expert_ids.shape[1]
    experts = NZ * NX
    cap = tok * top * 5 // (4 * experts)
    y, core = lax.axis_index("y"), lax.axis_index("core")
    z, x = lax.axis_index("z"), lax.axis_index("x")
    w_up, w_down = up_weight[0], down_weight[0]
    hid = w_up.shape[1]

    def first_side(index):
        return 1 - 2 * ((index + core) % 2)

    group = (jnp.array(MEMBERS, jnp.int32) * first_side(z)) % NZ
    group_at = ((group // PAIRS) ^ core) * PAIRS + group % PAIRS
    side_x, side_y = first_side(x), first_side(y)
    column = jnp.stack([0 * side_x, side_x, -side_x, 0 * side_x + 2]) % NX

    def share_at(side, places):
        turn = (column - y) % NY
        near = jnp.where(turn == side % NY, places[1], places[2])
        return jnp.where(turn == 0, places[0], jnp.where(turn == 2, places[3], near))

    table = jnp.concatenate([
        group_at,
        share_at(side_y, (2, 0, 3, 1)),
        share_at(-side_y, (2, 0, 3, 1)),
        share_at(side_y, (0, 1, 2, 3)),
        share_at(-side_y, (0, 1, 2, 3)),
    ]).astype(jnp.int32)

    ids_t, gates_t = expert_ids.T, gates.T
    meta = jnp.concatenate(
        [ids_t.astype(BF), *split3(gates_t), jnp.zeros((top, width - 4 * tok), BF)], axis=1
    )
    x_pairs = gather_z(
        jnp.concatenate([tokens, meta], axis=0),
        lambda a, b: jnp.concatenate([a[:tok], b[:tok], a[tok:], b[tok:]], axis=0),
    )
    c_pairs = gather_z(
        tie(cotangent, x_pairs[3]), lambda a, b: jnp.concatenate([a, b], axis=0)
    )

    meta = jnp.stack([q[2 * tok :, : 4 * tok] for q in x_pairs])
    meta = meta.reshape(NZ, top, 4 * tok)
    ids_d = meta[:, :, :tok].astype(F32)
    gates_d = sum(meta[:, :, i * tok : (i + 1) * tok].astype(F32) for i in (1, 2, 3))
    labels = (z * NX + (x + column) % NX).astype(F32)
    hit = ids_d[:, None] == labels[None, :, None, None]
    gate_of = jnp.sum(jnp.where(hit, gates_d[:, None], 0.0), axis=2)
    hit = hit.any(axis=2)
    rank = ranks_before(hit.reshape(NZ * NX, tok)).reshape(NZ, NX, tok)
    place = jnp.where(hit, rank, -1.0)

    def by_pair(value, fill):
        value = value.reshape(PAIRS, 2, NX, tok).transpose(0, 2, 1, 3)
        none = jnp.full_like(value, fill)
        return jnp.stack([
            jnp.concatenate([value[:, :, 0], none[:, :, 0]], axis=2),
            jnp.concatenate([none[:, :, 1], value[:, :, 1]], axis=2),
        ], axis=2)

    both = by_pair(place, -1.0)
    pick = both[:, :, :, None, :] == jnp.arange(cap, dtype=F32)[None, None, None, :, None]
    gate_rows = jnp.where(pick, by_pair(gate_of, 0.0)[:, :, :, None, :], 0.0)
    gate_rows = gate_rows.reshape(PAIRS, NX * 2 * cap, 2 * tok)
    pick = pick.astype(BF).reshape(PAIRS, NX * 2 * cap, 2 * tok)
    gate_hi = lax.reduce_precision(gate_rows, 8, 7)
    gate_lo = (gate_rows - gate_hi).astype(BF)
    gate_hi = gate_hi.astype(BF)

    def reduce(blocks, weight, contract):
        away = partial_sums(table, NZ + NX, 1, blocks, weight, contract, BF)
        got = swap_core(away)
        keep = partial_sums(table, NZ, 0, blocks, weight, contract, F32)
        near = swap((keep[:2] + got[:2].astype(F32)).astype(BF), "y", NY, 0)
        send = (keep[3] + got[3].astype(F32) + near[1].astype(F32)).astype(BF)
        last = swap(send, "y", NY, 1)
        return keep[2] + got[2].astype(F32) + near[0].astype(F32) + last.astype(F32)

    def spread(share):
        pair = jnp.stack([share, swap(share, "y", NY, 0)])
        far = swap(pair, "y", NY, 1)
        return [pair, far, swap_core(pair), swap_core(far)]

    x_recv = exchange(select_rows(table, pick, (), x_pairs, cap))
    c_recv = exchange(select_rows(table, pick, (gate_hi, gate_lo), c_pairs, cap))

    pre = reduce(x_recv, w_up, 0)
    logistic = jax.nn.sigmoid(pre)
    hidden_part = pre * logistic
    out_rows, hidden = expand_rows(table, NZ + 2 * NX, spread(hidden_part.astype(BF)), w_down, 0)
    out_recv = exchange(out_rows)

    raw = reduce(c_recv, w_down, 1)
    slot_gg = jnp.sum(hidden_part * raw, axis=1)
    grad_part = (raw * (logistic * (1.0 + pre * (1.0 - logistic)))).astype(BF)
    dx_rows, pre_grad = expand_rows(table, NZ + 2 * NX, spread(grad_part), w_up, 1)
    dx_recv = exchange([tie(r, *out_recv[1:3]) for r in dx_rows])

    mixed = sum_z(mix_rows(table, (gate_hi, gate_lo), out_recv, cap))
    input_grads = sum_z(mix_rows(table, (pick,), dx_recv, cap))

    down_grad = lax.dot_general(
        hidden, jnp.concatenate(c_recv, axis=0), (((0,), (0,)), ((), ())),
        preferred_element_type=F32,
    ).astype(BF)
    up_grad = lax.dot_general(
        jnp.concatenate(x_recv, axis=0), pre_grad, (((0,), (0,)), ((), ())),
        preferred_element_type=F32,
    ).astype(BF)

    zero_core = core == 0
    gg_pair = jnp.stack([slot_gg, swap(slot_gg, "y", NY, 0)])
    ring = jnp.concatenate([gg_pair, swap(gg_pair, "y", NY, 1)])
    away = swap_core(ring)
    def by_turn(value, side):
        up = side == 1
        return jnp.stack([value[0], jnp.where(up, value[1], value[2]), value[3],
                          jnp.where(up, value[2], value[1])])
    ring, away = by_turn(ring, side_y), by_turn(away, -side_y)
    ring = jnp.stack([jnp.where(zero_core, ring, away), jnp.where(zero_core, away, ring)], axis=1)
    by_dx = jnp.roll(ring, y, axis=0).reshape(NX, NZ, cap)
    by_group = jnp.roll(jnp.roll(by_dx, x, axis=0), z, axis=1)
    gg = by_group.transpose(1, 0, 2).reshape(experts, cap)
    gg = lax.all_to_all(gg, ("z", "x"), split_axis=0, concat_axis=0, tiled=True)
    own = ids_t[:, None, :] == jnp.arange(experts, dtype=jnp.int32)[None, :, None]
    token_hit = own.any(axis=0)
    token_place = jnp.where(token_hit, ranks_before(token_hit), -1.0)
    at = token_place[:, None, :] == jnp.arange(cap, dtype=F32)[None, :, None]
    value = jnp.sum(jnp.where(at, gg[:, :, None], 0.0), axis=1)
    gate_grads = (jnp.sum(jnp.where(own, value[None], 0.0), axis=1) / gates_t).T
    return mixed, input_grads, up_grad[None], down_grad[None], gate_grads


def solution(mesh):
    grid = Mesh(mesh.devices.reshape(NY, 2, NZ, NX), ("y", "core", "z", "x"))
    dp, ex = ("y", "core"), ("z", "x")
    return jax.shard_map(
        per_device,
        mesh=grid,
        in_specs=(P(ex, dp), P(ex, dp), P(ex, None), P(ex, None), P(ex, dp, None), P(ex, None, dp)),
        out_specs=(P(ex, dp), P(ex, dp), P(ex, dp, None), P(ex, None, dp), P(ex, None)),
        check_vma=False,
    )
```

```python
import jax
import jax.numpy as jnp
from jax import lax
from jax.experimental import pallas as pl
from jax.experimental.pallas import tpu as pltpu
from jax.sharding import Mesh
from jax.sharding import PartitionSpec as P

BF = jnp.bfloat16
F32 = jnp.float32

NZ, NX, NY = 8, 4, 4
PAIRS = NZ // 2
MEMBERS = (0, 1, -1, -2, 2, 3, -3, -4)


ANY = pl.BlockSpec(memory_space=pl.ANY)
VMEM = pl.BlockSpec(memory_space=pltpu.VMEM)
SMEM = pl.BlockSpec(memory_space=pltpu.SMEM)


def swap(value, axis, size, turn):
    pairs = []
    for c in range(2):
        for i in range(size):
            side = 1 if (i + (c if axis != "x" else 0) + turn) % 2 == 0 else -1
            to = (i + side) % size
            pairs.append((2 * i + c, 2 * to + c) if axis == "y" else (c * size + i, c * size + to))
    return lax.ppermute(value, ("y", "core") if axis == "y" else ("core", axis), pairs)


def swap_core(value):
    return lax.ppermute(value, "core", [(0, 1), (1, 0)])


def tie(value, *others):
    return lax.optimization_barrier((value, *others))[0]


def gather_z(block, join, after=()):
    first = swap(block, "z", NZ, 0)
    pairs = [join(block, first)]
    if after:
        pairs[0] = tie(pairs[0], *after)
    for turn in (1, 0, 1):
        pairs.append(swap(pairs[-1], "z", NZ, turn))
    return pairs


def sum_z(parts):
    tok = parts[0].shape[0] // 2
    total = parts[3]
    for k, turn in ((2, 1), (1, 0), (0, 1)):
        got = swap(total, "z", NZ, turn)
        if k:
            total = (parts[k].astype(F32) + got.astype(F32)).astype(BF)
    last = (parts[0][tok:].astype(F32) + got[tok:].astype(F32)).astype(BF)
    end = swap(last, "z", NZ, 0)
    return (parts[0][:tok].astype(F32) + got[:tok].astype(F32) + end.astype(F32)).astype(BF)


def exchange(blocks):
    own, first, second, opposite = blocks
    far = swap(opposite, "x", NX, 0)
    from_first = swap(first, "x", NX, 0)
    from_second = swap(second, "x", NX, 1)
    from_opposite = swap(far, "x", NX, 1)
    return [own, from_first, from_second, from_opposite]


def select_rows(table, pick, weights, pairs, cap):
    tok2, width = pick.shape[2], pairs[0].shape[1]
    scaled = bool(weights)
    pieces = NX * 2

    def kernel(table_ref, pick_ref, *refs):
        weight_refs, refs = refs[: len(weights)], refs[len(weights) :]
        blocks, outs, (held, made, sems, out_sems) = (
            refs[:PAIRS], refs[PAIRS : PAIRS + NX], refs[PAIRS + NX :]
        )
        k = pl.program_id(0)

        def put(at, n):
            return pltpu.make_async_copy(
                made.at[at, n], outs[n // 2].at[table_ref[2 * at + n % 2]], out_sems.at[at, n]
            )

        @pl.when(k == 0)
        def _():
            for m in range(PAIRS):
                pltpu.make_async_copy(
                    blocks[m].at[pl.ds(0, tok2)], held.at[m], sems.at[m]
                ).start()

        pltpu.make_async_copy(blocks[0].at[pl.ds(0, tok2)], held.at[k], sems.at[k]).wait()
        rows = jnp.dot(pick_ref[0], held[k], preferred_element_type=F32)
        if scaled:
            rows = rows * sum(
                jnp.sum(w[0].astype(F32), axis=1, keepdims=True) for w in weight_refs
            )
        for n in range(pieces):
            made[k, n] = rows[n * cap : (n + 1) * cap].astype(BF)
        for n in range(pieces):
            put(k, n).start()

        @pl.when(k == PAIRS - 1)
        def _():
            def finish(at, carry):
                for n in range(pieces):
                    put(at, n).wait()
                return carry

            lax.fori_loop(0, PAIRS, finish, 0)

    per_pair = pl.BlockSpec((1, pick.shape[1], tok2), lambda k: (k, 0, 0))
    outs = pl.pallas_call(
        kernel,
        grid=(PAIRS,),
        out_shape=[jax.ShapeDtypeStruct((NZ, cap, width), BF)] * NX,
        in_specs=[SMEM, per_pair] + [per_pair] * len(weights) + [ANY] * PAIRS,
        out_specs=[ANY] * NX,
        scratch_shapes=[
            pltpu.VMEM((PAIRS, tok2, width), BF),
            pltpu.VMEM((PAIRS, pieces, cap, width), BF),
            pltpu.SemaphoreType.DMA((PAIRS,)),
            pltpu.SemaphoreType.DMA((PAIRS, pieces)),
        ],
        cost_estimate=pl.CostEstimate(
            flops=600_000_000, bytes_accessed=5_000_000, transcendentals=0
        ),
        name="select_scaled" if scaled else "select_plain",
    )(table, pick, *weights, *pairs)
    return [o.reshape(NZ * cap, width) for o in outs]


def mix_rows(table, picks, rows, cap):
    tok2, width = picks[0].shape[2], rows[0].shape[1]
    rows = [r.reshape(NZ, cap, width) for r in rows]
    pieces = NX * 2

    def kernel(table_ref, *refs):
        pick_refs, refs = refs[: len(picks)], refs[len(picks) :]
        blocks, outs, (held, made, sems, out_sems) = (
            refs[:NX], refs[NX : NX + PAIRS], refs[NX + PAIRS :]
        )
        step = pl.program_id(0)
        k = PAIRS - 1 - step

        def get(at, n):
            return pltpu.make_async_copy(
                blocks[n // 2].at[table_ref[2 * at + n % 2]], held.at[at, n], sems.at[at, n]
            )

        @pl.when(step == 0)
        def _():
            def begin(at, carry):
                for n in range(pieces):
                    get(PAIRS - 1 - at, n).start()
                return carry

            lax.fori_loop(0, PAIRS, begin, 0)

        for n in range(pieces):
            get(k, n).wait()
        stack = jnp.concatenate(
            [held[k, n].astype(F32) for n in range(pieces)], axis=0
        ).astype(BF)
        total = None
        for ref in pick_refs:
            part = lax.dot_general(
                ref[0], stack, (((0,), (0,)), ((), ())), preferred_element_type=F32
            )
            total = part if total is None else total + part
        made[k] = total.astype(BF)
        puts = [pltpu.make_async_copy(made.at[m], outs[m], out_sems.at[m]) for m in range(PAIRS)]
        for m in range(PAIRS):
            pl.when(k == m)(puts[m].start)

        @pl.when(k == 0)
        def _():
            for put in puts:
                put.wait()

    per_pair = pl.BlockSpec((1, picks[0].shape[1], tok2), lambda n: (PAIRS - 1 - n, 0, 0))
    return pl.pallas_call(
        kernel,
        grid=(PAIRS,),
        out_shape=[jax.ShapeDtypeStruct((tok2, width), BF)] * PAIRS,
        in_specs=[SMEM] + [per_pair] * len(picks) + [ANY] * NX,
        out_specs=[ANY] * PAIRS,
        scratch_shapes=[
            pltpu.VMEM((PAIRS, pieces, cap, width), BF),
            pltpu.VMEM((PAIRS, tok2, width), BF),
            pltpu.SemaphoreType.DMA((PAIRS, pieces)),
            pltpu.SemaphoreType.DMA((PAIRS,)),
        ],
        cost_estimate=pl.CostEstimate(
            flops=600_000_000 * len(picks), bytes_accessed=5_000_000, transcendentals=0
        ),
        name="mix%d" % len(picks),
    )(table, *picks, *rows)


def partial_sums(table, offset, blocks, weight, contract):
    rows, width = blocks[0].shape[0] // 2, blocks[0].shape[1]
    hid = weight.shape[1 - contract]
    step = 256

    def kernel(table_ref, weight_ref, *refs):
        ins, (keep, away, held, sems) = refs[:NX], refs[NX:]

        @pl.when(pl.program_id(0) == 0)
        def _():
            copies = [
                pltpu.make_async_copy(ins[i], held.at[pl.ds(i * 2 * rows, 2 * rows)], sems.at[i])
                for i in range(NX)
            ]
            for c in copies:
                c.start()
            for c in copies:
                c.wait()

        made = lax.dot_general(
            held[...], weight_ref[...], (((1,), (contract,)), ((), ())),
            preferred_element_type=F32,
        )
        for i in range(NX):
            at = i * 2 * rows
            keep[table_ref[offset + i]] = made[at : at + rows]
            away[table_ref[offset + NX + i]] = made[at + rows : at + 2 * rows].astype(BF)

    if contract == 0:
        weight_spec = pl.BlockSpec((width, step), lambda n: (0, n))
    else:
        weight_spec = pl.BlockSpec((step, width), lambda n: (n, 0))
    out_spec = pl.BlockSpec((NX, rows, step), lambda n: (0, 0, n))
    return pl.pallas_call(
        kernel,
        grid=(hid // step,),
        out_shape=[
            jax.ShapeDtypeStruct((NX, rows, hid), F32), jax.ShapeDtypeStruct((NX, rows, hid), BF)
        ],
        in_specs=[SMEM, weight_spec] + [ANY] * NX,
        out_specs=[out_spec] * 2,
        scratch_shapes=[pltpu.VMEM((NX * 2 * rows, width), BF), pltpu.SemaphoreType.DMA((NX,))],
        cost_estimate=pl.CostEstimate(
            flops=2_400_000_000, bytes_accessed=9_000_000, transcendentals=0
        ),
        name="partial%d" % contract,
    )(table, weight, *blocks)


def expand_rows(table, offset, shares, rows, weight, contract):
    hid, width = weight.shape[contract], weight.shape[1 - contract]

    def kernel(table_ref, weight_ref, *refs):
        ins, refs = refs[:4], refs[4:]
        outs, joined, (held, made, in_sems, out_sems, join_sems) = (
            refs[:NX], refs[NX], refs[NX + 1 :]
        )
        for n in range(4):
            for m in range(2):
                place = table_ref[offset + 2 * n + m]
                pltpu.make_async_copy(
                    ins[n].at[m, :, pl.ds(0, hid)], held.at[place, n // 2], in_sems.at[place, n // 2]
                ).start()
        puts = [pltpu.make_async_copy(made.at[i], outs[i], out_sems.at[i]) for i in range(NX)]

        def keep(i):
            return pltpu.make_async_copy(held.at[i], joined.at[i], join_sems.at[i])

        def step(n, carry):
            i = NX - 1 - n
            for h in range(2):
                pltpu.make_async_copy(
                    ins[0].at[0, :, pl.ds(0, hid)], held.at[i, h], in_sems.at[i, h]
                ).wait()
            keep(i).start()
            made[i] = lax.dot_general(
                held[i].reshape(2 * rows, hid), weight_ref[...],
                (((1,), (contract,)), ((), ())), preferred_element_type=F32,
            ).astype(BF)
            for m in range(NX):
                pl.when(i == m)(puts[m].start)
            return carry

        lax.fori_loop(0, NX, step, 0)
        for put in puts:
            put.wait()
        for i in range(NX):
            keep(i).wait()

    *outs, joined = pl.pallas_call(
        kernel,
        out_shape=[jax.ShapeDtypeStruct((2 * rows, width), BF)] * NX
        + [jax.ShapeDtypeStruct((NX, 2, rows, hid), BF)],
        in_specs=[SMEM, VMEM] + [ANY] * 4,
        out_specs=[ANY] * (NX + 1),
        scratch_shapes=[
            pltpu.VMEM((NX, 2, rows, hid), BF),
            pltpu.VMEM((NX, 2 * rows, width), BF),
            pltpu.SemaphoreType.DMA((NX, 2)),
            pltpu.SemaphoreType.DMA((NX,)),
            pltpu.SemaphoreType.DMA((NX,)),
        ],
        cost_estimate=pl.CostEstimate(
            flops=2_400_000_000, bytes_accessed=9_000_000, transcendentals=0
        ),
        name="expand%d" % contract,
    )(table, weight, *shares)
    return outs, joined.reshape(NX * 2 * rows, hid)


def weight_grads(left, blocks, joined_left, name):
    slots, hid = left.shape
    each, width = blocks[0].shape
    step = 256 if joined_left else 128
    count = (hid if joined_left else width) // step

    def kernel(left_ref, *refs):
        ins, (out, held, sems) = refs[:NX], refs[NX:]

        @pl.when(pl.program_id(0) == 0)
        def _():
            copies = [
                pltpu.make_async_copy(ins[i], held.at[pl.ds(i * each, each)], sems.at[i])
                for i in range(NX)
            ]
            for c in copies:
                c.start()
            for c in copies:
                c.wait()

        if joined_left:
            a, b = left_ref[...], held[...]
        else:
            at = pl.multiple_of(pl.program_id(0) * step, step)
            a, b = held[:, pl.ds(at, step)], left_ref[...]
        out[...] = lax.dot_general(
            a, b, (((0,), (0,)), ((), ())), preferred_element_type=F32
        ).astype(BF)

    if joined_left:
        left_spec, shape = pl.BlockSpec((slots, step), lambda n: (0, n)), (hid, width)
    else:
        left_spec, shape = pl.BlockSpec((slots, hid), lambda n: (0, 0)), (width, hid)
    return pl.pallas_call(
        kernel,
        grid=(count,),
        out_shape=jax.ShapeDtypeStruct(shape, BF),
        in_specs=[left_spec] + [ANY] * NX,
        out_specs=pl.BlockSpec((step, shape[1]), lambda n: (n, 0)),
        scratch_shapes=[pltpu.VMEM((slots, width), BF), pltpu.SemaphoreType.DMA((NX,))],
        cost_estimate=pl.CostEstimate(
            flops=2_400_000_000, bytes_accessed=7_000_000, transcendentals=0
        ),
        name=name,
    )(left, *blocks)


def route(table, offset, pairs, cap):
    tok2, tok = 256, 128
    top, width = (pairs[0].shape[0] - tok2) // 2, pairs[0].shape[1]
    rows = NX * 2 * cap

    def kernel(table_ref, *refs):
        blocks, (pick_ref, hi_ref, lo_ref, held, sems) = refs[:PAIRS], refs[PAIRS:]
        k = pl.program_id(0)

        def get(m, at):
            return pltpu.make_async_copy(
                blocks[m].at[pl.ds(tok2, 2 * top)], held.at[at], sems.at[at]
            )

        @pl.when(k == 0)
        def _():
            for m in range(PAIRS):
                get(m, m).start()

        get(0, k).wait()
        meta = held[k].astype(F32)
        chosen, weight = [], []
        for i in range(NX):
            label = table_ref[offset + i].astype(F32)
            for j in range(2):
                part = meta[j * top : (j + 1) * top]
                gates = part[:, tok : 2 * tok] + part[:, 2 * tok : 3 * tok] + part[:, 3 * tok : 4 * tok]
                hit = (part[:, :tok] == label).astype(F32)
                chosen.append(jnp.sum(hit, axis=0, keepdims=True))
                weight.append(jnp.sum(hit * gates, axis=0, keepdims=True))
        chosen = jnp.concatenate(chosen, axis=0)
        earlier = lax.broadcasted_iota(jnp.int32, (tok, tok), 0)
        later = lax.broadcasted_iota(jnp.int32, (tok, tok), 1)
        strict = jnp.where(earlier < later, 1.0, 0.0).astype(BF)
        rank = jnp.dot(chosen.astype(BF), strict, preferred_element_type=F32)
        place = jnp.where(chosen > 0.0, rank, -1.0)
        slot = lax.broadcasted_iota(jnp.int32, (cap, tok), 0).astype(F32)
        none = jnp.zeros((cap, tok), F32)
        for n in range(NX * 2):
            here = slot == place[n : n + 1]
            one = jnp.where(here, 1.0, 0.0)
            gate = jnp.where(here, jnp.broadcast_to(weight[n], (cap, tok)), 0.0)
            high = gate.astype(BF)
            low = gate - high.astype(F32)
            for ref, value in ((pick_ref, one), (hi_ref, high.astype(F32)), (lo_ref, low)):
                both = [value, none] if n % 2 == 0 else [none, value]
                ref[0, n * cap : (n + 1) * cap] = jnp.concatenate(both, axis=1).astype(BF)

    return pl.pallas_call(
        kernel,
        grid=(PAIRS,),
        out_shape=[jax.ShapeDtypeStruct((PAIRS, rows, tok2), BF)] * 3,
        in_specs=[SMEM] + [ANY] * PAIRS,
        out_specs=[pl.BlockSpec((1, rows, tok2), lambda k: (k, 0, 0))] * 3,
        scratch_shapes=[pltpu.VMEM((PAIRS, 2 * top, width), BF), pltpu.SemaphoreType.DMA((PAIRS,))],
        cost_estimate=pl.CostEstimate(flops=10_000_000, bytes_accessed=2_000_000, transcendentals=0),
        name="route",
    )(table, *pairs)


def grad_share(keep, got, near, last, pre):
    rows, hid = pre.shape
    step = 16

    def kernel(keep_ref, got_ref, near_ref, last_ref, pre_ref, out):
        def body(n, carry):
            at = pl.ds(pl.multiple_of(n * step, step), step)
            raw = keep_ref[0, at].astype(F32) + got_ref[0, at].astype(F32)
            raw = raw + near_ref[0, at].astype(F32) + last_ref[at].astype(F32)
            pre = pre_ref[at]
            logistic = 1.0 / (1.0 + jnp.exp(-pre))
            out[at, :hid] = (raw * (logistic * (1.0 + pre * (1.0 - logistic)))).astype(BF)
            gate = jnp.sum(pre * logistic * raw, axis=1, keepdims=True)
            high = gate.astype(BF).astype(F32)
            mid = (gate - high).astype(BF).astype(F32)
            low = gate - high - mid
            lane = lax.broadcasted_iota(jnp.int32, (step, 128), 1)
            tail = jnp.where(lane == 0, high, jnp.where(lane == 1, mid, jnp.where(lane == 2, low, 0.0)))
            out[at, hid:] = tail.astype(BF)
            return carry

        lax.fori_loop(0, rows // step, body, 0)

    return pl.pallas_call(
        kernel,
        grid=(1,),
        out_shape=jax.ShapeDtypeStruct((rows, hid + 128), BF),
        in_specs=[
            pl.BlockSpec((1, rows, hid), lambda n: (2, 0, 0)),
            pl.BlockSpec((1, rows, hid), lambda n: (2, 0, 0)),
            pl.BlockSpec((1, rows, hid), lambda n: (0, 0, 0)),
            pl.BlockSpec((rows, hid), lambda n: (0, 0)),
            pl.BlockSpec((rows, hid), lambda n: (0, 0)),
        ],
        out_specs=pl.BlockSpec((rows, hid + 128), lambda n: (0, 0)),
        cost_estimate=pl.CostEstimate(flops=3_000_000, bytes_accessed=3_000_000, transcendentals=200_000),
        name="grad_share",
    )(keep, got, near, last, pre)


def pack_kernel(tokens_ref, ids_ref, gates_ref, out):
    tok, width = tokens_ref.shape
    top = ids_ref.shape[0]
    out[:tok] = tokens_ref[...]
    gates = gates_ref[...]
    hi = gates.astype(BF)
    mid = (gates - hi.astype(F32)).astype(BF)
    low = (gates - hi.astype(F32) - mid.astype(F32)).astype(BF)
    rest = jnp.zeros((top, width - 4 * tok), BF)
    out[tok:] = jnp.concatenate([ids_ref[...].astype(F32).astype(BF), hi, mid, low, rest], axis=1)


def ranks_before(chosen):
    count = chosen.shape[-1]
    earlier = lax.broadcasted_iota(jnp.int32, (count, count), 0)
    later = lax.broadcasted_iota(jnp.int32, (count, count), 1)
    strict = (earlier < later).astype(BF)
    return jnp.dot(chosen.astype(BF), strict, preferred_element_type=F32)


def per_device(tokens, cotangent, expert_ids, gates, up_weight, down_weight):
    tok, width = tokens.shape
    top = expert_ids.shape[1]
    experts = NZ * NX
    cap = tok * top * 5 // (4 * experts)
    y, core = lax.axis_index("y"), lax.axis_index("core")
    z, x = lax.axis_index("z"), lax.axis_index("x")
    w_up, w_down = up_weight[0], down_weight[0]
    hid = w_up.shape[1]

    def first_side(index):
        return 1 - 2 * (index % 2)

    group = (jnp.array(MEMBERS, jnp.int32) * first_side(z + core)) % NZ
    group_at = ((group // PAIRS) ^ core) * PAIRS + group % PAIRS
    side_x, side_y = first_side(x), first_side(y + core)
    column = jnp.stack([0 * side_x, side_x, -side_x, 0 * side_x + 2]) % NX

    def share_at(side, places):
        turn = (column - y) % NY
        near = jnp.where(turn == side % NY, places[1], places[2])
        return jnp.where(turn == 0, places[0], jnp.where(turn == 2, places[3], near))

    def inverse(order):
        count = jnp.arange(NX, dtype=jnp.int32)
        return jnp.sum(jnp.where(order[None, :] == count[:, None], count[None, :], 0), axis=1)

    table = jnp.concatenate([
        group_at,
        share_at(side_y, (2, 0, 3, 1)),
        share_at(-side_y, (2, 0, 3, 1)),
        inverse(share_at(side_y, (0, 1, 2, 3))),
        inverse(share_at(-side_y, (0, 1, 2, 3))),
        z * NX + (x + column) % NX,
    ]).astype(jnp.int32)

    ids_t, gates_t = expert_ids.T, gates.T
    packed = pl.pallas_call(
        pack_kernel,
        out_shape=jax.ShapeDtypeStruct((tok + top, width), BF),
        in_specs=[VMEM] * 3,
        out_specs=VMEM,
        name="pack",
    )(tokens, ids_t, gates_t)
    x_pairs = gather_z(
        packed,
        lambda a, b: jnp.concatenate([a[:tok], b[:tok], a[tok:], b[tok:]], axis=0),
    )

    pick, gate_hi, gate_lo = route(table, NZ + 4 * NX, x_pairs, cap)

    def reduce(blocks, weight, contract, before=(), ahead=()):
        if before:
            blocks = [tie(blocks[0], *before), *blocks[1:]]
        keep, away = partial_sums(table, NZ, blocks, weight, contract)
        got = swap_core(away)
        send = (keep[:2] + got[:2].astype(F32)).astype(BF)
        near = swap(tie(send, *ahead) if ahead else send, "y", NY, 0)
        send = (keep[3] + got[3].astype(F32) + near[1].astype(F32)).astype(BF)
        return keep, got, near, swap(send, "y", NY, 1), send

    def spread(share):
        pair = jnp.stack([share, swap(share, "y", NY, 0)])
        far = swap(pair, "y", NY, 1)
        return [pair, far, swap_core(pair), swap_core(far)]

    x_rows = select_rows(table, pick, (), x_pairs, cap)
    x_recv = exchange(x_rows)
    c_pairs = gather_z(
        tie(cotangent, x_pairs[2]), lambda a, b: jnp.concatenate([a, b], axis=0), x_rows[:1]
    )
    c_rows = select_rows(table, pick, (gate_hi, gate_lo), c_pairs, cap)
    c_recv = exchange([tie(r, *x_recv[1:3]) for r in c_rows])

    keep, got, near, last, sent = reduce(x_recv, w_up, 0)
    pre = keep[2] + got[2].astype(F32) + near[0].astype(F32) + last.astype(F32)
    logistic = jax.nn.sigmoid(pre)
    hidden_part = pre * logistic
    share = hidden_part.shape[0]
    hidden_part = hidden_part.astype(BF)
    out_rows, hidden = expand_rows(table, NZ + 2 * NX, spread(hidden_part), share, w_down, 0)
    out_recv = exchange(out_rows)

    keep, got, near, last, _ = reduce(c_recv, w_down, 1, (sent,), (hidden_part,))
    grads = spread(grad_share(keep, got, near, last, pre))
    dx_rows, pre_grad = expand_rows(table, NZ + 2 * NX, grads, share, w_up, 1)
    dx_recv = exchange([tie(r, *out_recv[1:3]) for r in dx_rows])

    mixed = sum_z(mix_rows(table, (gate_hi, gate_lo), out_recv, cap))
    dx_parts = list(mix_rows(table, (pick,), dx_recv, cap))
    down_grad = weight_grads(tie(hidden, dx_parts[0]), c_recv, True, "down_grads")
    dx_parts[1] = tie(dx_parts[1], down_grad)
    up_grad = weight_grads(tie(pre_grad, down_grad), x_recv, False, "up_grads")
    dx_parts[0] = tie(dx_parts[0], up_grad)
    input_grads = sum_z(dx_parts)

    zero_core = core == 0
    def slot_values(pair):
        return jnp.sum(pair[:, :, hid : hid + 3].astype(F32), axis=2)

    ring = jnp.concatenate([slot_values(grads[0]), slot_values(grads[1])])
    away = jnp.concatenate([slot_values(grads[2]), slot_values(grads[3])])

    def by_turn(value, side):
        up = side == 1
        return jnp.stack([value[0], jnp.where(up, value[1], value[2]), value[3],
                          jnp.where(up, value[2], value[1])])
    ring, away = by_turn(ring, side_y), by_turn(away, -side_y)
    ring = jnp.stack([jnp.where(zero_core, ring, away), jnp.where(zero_core, away, ring)], axis=1)
    by_dx = jnp.roll(ring, y, axis=0).reshape(NX, NZ, cap)
    by_group = jnp.roll(jnp.roll(by_dx, x, axis=0), z, axis=1)
    gg = tie(by_group.transpose(1, 0, 2).reshape(experts, cap), dx_recv[1])
    gg = lax.all_to_all(gg, ("z", "x"), split_axis=0, concat_axis=0, tiled=True)
    own = ids_t[:, None, :] == jnp.arange(experts, dtype=jnp.int32)[None, :, None]
    token_hit = own.any(axis=0)
    token_place = jnp.where(token_hit, ranks_before(token_hit), -1.0)
    at = token_place[:, None, :] == jnp.arange(cap, dtype=F32)[None, :, None]
    value = jnp.sum(jnp.where(at, gg[:, :, None], 0.0), axis=1)
    gate_grads = (jnp.sum(jnp.where(own, value[None], 0.0), axis=1) / gates_t).T
    return mixed, input_grads, up_grad[None], down_grad[None], gate_grads


def solution(mesh):
    grid = Mesh(mesh.devices.reshape(NY, 2, NZ, NX), ("y", "core", "z", "x"))
    dp, ex = ("y", "core"), ("z", "x")
    return jax.shard_map(
        per_device,
        mesh=grid,
        in_specs=(P(ex, dp), P(ex, dp), P(ex, None), P(ex, None), P(ex, dp, None), P(ex, None, dp)),
        out_specs=(P(ex, dp), P(ex, dp), P(ex, dp, None), P(ex, None, dp), P(ex, None)),
        check_vma=False,
    )
```

```python
import jax
import jax.numpy as jnp
from jax import lax
from jax.experimental import pallas as pl
from jax.experimental.pallas import tpu as pltpu
from jax.sharding import Mesh
from jax.sharding import PartitionSpec as P

BF = jnp.bfloat16
F32 = jnp.float32

NZ, NX, NY = 8, 4, 4
CHUNKS = 4


ANY = pl.BlockSpec(memory_space=pl.ANY)
VMEM = pl.BlockSpec(memory_space=pltpu.VMEM)
SMEM = pl.BlockSpec(memory_space=pltpu.SMEM)


def swap(value, turn):
    pairs = []
    for c in range(2):
        for i in range(NY):
            side = 1 if (i + c + turn) % 2 == 0 else -1
            pairs.append((2 * i + c, 2 * ((i + side) % NY) + c))
    return lax.ppermute(value, ("y", "core"), pairs)


def swap_core(value):
    return lax.ppermute(value, "core", [(0, 1), (1, 0)])


def tie(value, *others):
    return lax.optimization_barrier((value, *others))[0]


def scatter(rows):
    parts = rows.reshape(NZ * NX, rows.shape[0] // (NZ * NX), rows.shape[1])
    parts = lax.all_to_all(parts, ("z", "x"), split_axis=0, concat_axis=0, tiled=True)
    return parts.reshape(rows.shape)


def select_rows(pick, weights, values):
    slots, tok = pick.shape
    width = values.shape[1]
    step = slots // CHUNKS

    def kernel(pick_ref, *refs):
        weight_refs, (values_ref, out) = refs[: len(weights)], refs[len(weights) :]
        rows = jnp.dot(pick_ref[...], values_ref[...], preferred_element_type=F32)
        if weights:
            rows = rows * sum(
                jnp.sum(w[...].astype(F32), axis=1, keepdims=True) for w in weight_refs
            )
        out[...] = rows.astype(BF)

    chunk = pl.BlockSpec((step, tok), lambda k: (k, 0))
    return pl.pallas_call(
        kernel,
        grid=(CHUNKS,),
        out_shape=jax.ShapeDtypeStruct((slots, width), BF),
        in_specs=[chunk] * (1 + len(weights)) + [pl.BlockSpec((tok, width), lambda k: (0, 0))],
        out_specs=pl.BlockSpec((step, width), lambda k: (k, 0)),
        cost_estimate=pl.CostEstimate(flops=300_000_000, bytes_accessed=3_000_000, transcendentals=0),
        name="select_scaled" if weights else "select_plain",
    )(pick, *weights, values)


def mix_rows(picks, rows):
    slots, tok = picks[0].shape
    width = rows.shape[1]
    step = slots // CHUNKS

    def kernel(*refs):
        pick_refs, (rows_ref, out, total) = refs[: len(picks)], refs[len(picks) :]
        k = pl.program_id(0)

        @pl.when(k == 0)
        def _():
            total[...] = jnp.zeros_like(total)

        for ref in pick_refs:
            total[...] += lax.dot_general(
                ref[...], rows_ref[...], (((0,), (0,)), ((), ())), preferred_element_type=F32
            )

        @pl.when(k == CHUNKS - 1)
        def _():
            out[...] = total[...].astype(BF)

    return pl.pallas_call(
        kernel,
        grid=(CHUNKS,),
        out_shape=jax.ShapeDtypeStruct((tok, width), BF),
        in_specs=[pl.BlockSpec((step, tok), lambda k: (k, 0))] * len(picks)
        + [pl.BlockSpec((step, width), lambda k: (k, 0))],
        out_specs=pl.BlockSpec((tok, width), lambda k: (0, 0)),
        scratch_shapes=[pltpu.VMEM((tok, width), F32)],
        cost_estimate=pl.CostEstimate(
            flops=300_000_000 * len(picks), bytes_accessed=3_000_000, transcendentals=0
        ),
        name="mix%d" % len(picks),
    )(*picks, rows)


def partial_sums(table, slot_rows, weight, contract):
    slots, width = slot_rows.shape
    rows = slots // (2 * NY)
    hid = weight.shape[1 - contract]
    step = 256

    def kernel(table_ref, weight_ref, rows_ref, keep, away, held, sems):
        @pl.when(pl.program_id(0) == 0)
        def _():
            core = table_ref[4 * NY]
            copies = [
                pltpu.make_async_copy(
                    rows_ref.at[i, h ^ core], held.at[pl.ds((2 * i + h) * rows, rows)], sems.at[i, h]
                )
                for i in range(NY)
                for h in range(2)
            ]
            for c in copies:
                c.start()
            for c in copies:
                c.wait()

        made = lax.dot_general(
            held[...], weight_ref[...], (((1,), (contract,)), ((), ())),
            preferred_element_type=F32,
        )
        for i in range(NY):
            at = i * 2 * rows
            keep[table_ref[i]] = made[at : at + rows]
            away[table_ref[NY + i]] = made[at + rows : at + 2 * rows].astype(BF)

    if contract == 0:
        weight_spec = pl.BlockSpec((width, step), lambda n: (0, n))
    else:
        weight_spec = pl.BlockSpec((step, width), lambda n: (n, 0))
    out_spec = pl.BlockSpec((NY, rows, step), lambda n: (0, 0, n))
    return pl.pallas_call(
        kernel,
        grid=(hid // step,),
        out_shape=[
            jax.ShapeDtypeStruct((NY, rows, hid), F32), jax.ShapeDtypeStruct((NY, rows, hid), BF)
        ],
        in_specs=[SMEM, weight_spec, ANY],
        out_specs=[out_spec] * 2,
        scratch_shapes=[pltpu.VMEM((slots, width), BF), pltpu.SemaphoreType.DMA((NY, 2))],
        cost_estimate=pl.CostEstimate(
            flops=2_400_000_000, bytes_accessed=9_000_000, transcendentals=0
        ),
        name="partial%d" % contract,
    )(table, weight, slot_rows.reshape(NY, 2, rows, width))


def expand_rows(table, shares, weight, contract):
    rows = shares[0].shape[1]
    hid, width = weight.shape[contract], weight.shape[1 - contract]

    def kernel(table_ref, weight_ref, *refs):
        ins, (out, joined, held, made, in_sems, out_sems, join_sems) = refs[:4], refs[4:]
        core = table_ref[4 * NY]
        for n in range(4):
            for m in range(2):
                place = table_ref[2 * NY + 2 * n + m]
                half = core if n < 2 else 1 - core
                pltpu.make_async_copy(
                    ins[n].at[m, :, pl.ds(0, hid)], held.at[place, half], in_sems.at[place, half]
                ).start()

        def put(i):
            return pltpu.make_async_copy(made.at[i], out.at[i], out_sems.at[i])

        def keep(i):
            return pltpu.make_async_copy(held.at[i], joined.at[i], join_sems.at[i])

        def step(i, carry):
            for h in range(2):
                pltpu.make_async_copy(
                    ins[0].at[0, :, pl.ds(0, hid)], held.at[i, h], in_sems.at[i, h]
                ).wait()
            keep(i).start()
            made[i] = lax.dot_general(
                held[i].reshape(2 * rows, hid), weight_ref[...],
                (((1,), (contract,)), ((), ())), preferred_element_type=F32,
            ).astype(BF)
            put(i).start()
            return carry

        lax.fori_loop(0, NY, step, 0)
        for i in range(NY):
            put(i).wait()
            keep(i).wait()

    out, joined = pl.pallas_call(
        kernel,
        out_shape=[
            jax.ShapeDtypeStruct((NY, 2 * rows, width), BF),
            jax.ShapeDtypeStruct((NY, 2, rows, hid), BF),
        ],
        in_specs=[SMEM, VMEM] + [ANY] * 4,
        out_specs=[ANY] * 2,
        scratch_shapes=[
            pltpu.VMEM((NY, 2, rows, hid), BF),
            pltpu.VMEM((NY, 2 * rows, width), BF),
            pltpu.SemaphoreType.DMA((NY, 2)),
            pltpu.SemaphoreType.DMA((NY,)),
            pltpu.SemaphoreType.DMA((NY,)),
        ],
        cost_estimate=pl.CostEstimate(
            flops=2_400_000_000, bytes_accessed=9_000_000, transcendentals=0
        ),
        name="expand%d" % contract,
    )(table, weight, *shares)
    return out.reshape(NY * 2 * rows, width), joined.reshape(NY * 2 * rows, hid)


def weight_grads(left, right, step, name):
    slots, count = left.shape
    width = right.shape[1]

    def kernel(left_ref, right_ref, out):
        out[...] = lax.dot_general(
            left_ref[...], right_ref[...], (((0,), (0,)), ((), ())), preferred_element_type=F32
        ).astype(BF)

    return pl.pallas_call(
        kernel,
        grid=(count // step,),
        out_shape=jax.ShapeDtypeStruct((count, width), BF),
        in_specs=[
            pl.BlockSpec((slots, step), lambda n: (0, n)),
            pl.BlockSpec((slots, width), lambda n: (0, 0)),
        ],
        out_specs=pl.BlockSpec((step, width), lambda n: (n, 0)),
        cost_estimate=pl.CostEstimate(
            flops=2_400_000_000, bytes_accessed=7_000_000, transcendentals=0
        ),
        name=name,
    )(left, right)


def route_kernel(ids_ref, gates_ref, pick_ref, hi_ref, lo_ref):
    tok = ids_ref.shape[1]
    each = 8
    cap = pick_ref.shape[0] // each
    chosen, weight = [], []
    for n in range(each):
        hit = jnp.where(ids_ref[...] == pl.program_id(0) * each + n, 1.0, 0.0)
        chosen.append(jnp.sum(hit, axis=0, keepdims=True))
        weight.append(jnp.sum(hit * gates_ref[...], axis=0, keepdims=True))
    chosen = jnp.concatenate(chosen, axis=0)
    earlier = lax.broadcasted_iota(jnp.int32, (tok, tok), 0)
    later = lax.broadcasted_iota(jnp.int32, (tok, tok), 1)
    strict = jnp.where(earlier < later, 1.0, 0.0).astype(BF)
    rank = jnp.dot(chosen.astype(BF), strict, preferred_element_type=F32)
    place = jnp.where(chosen > 0.0, rank, -1.0)
    slot = lax.broadcasted_iota(jnp.int32, (cap, tok), 0).astype(F32)
    one, high, low = [], [], []
    for n in range(each):
        here = slot == place[n : n + 1]
        gate = jnp.where(here, jnp.broadcast_to(weight[n], (cap, tok)), 0.0)
        one.append(jnp.where(here, 1.0, 0.0))
        high.append(gate.astype(BF).astype(F32))
        low.append(gate - high[-1])
    pick_ref[...] = jnp.concatenate(one, axis=0).astype(BF)
    hi_ref[...] = jnp.concatenate(high, axis=0).astype(BF)
    lo_ref[...] = jnp.concatenate(low, axis=0).astype(BF)


def grad_share(keep, got, near, last, pre):
    rows, hid = pre.shape
    step = 16

    def kernel(keep_ref, got_ref, near_ref, last_ref, pre_ref, out):
        def body(n, carry):
            at = pl.ds(pl.multiple_of(n * step, step), step)
            raw = keep_ref[0, at].astype(F32) + got_ref[0, at].astype(F32)
            raw = raw + near_ref[0, at].astype(F32) + last_ref[at].astype(F32)
            pre = pre_ref[at]
            logistic = 1.0 / (1.0 + jnp.exp(-pre))
            out[at, :hid] = (raw * (logistic * (1.0 + pre * (1.0 - logistic)))).astype(BF)
            gate = jnp.sum(pre * logistic * raw, axis=1, keepdims=True)
            high = gate.astype(BF).astype(F32)
            mid = (gate - high).astype(BF).astype(F32)
            low = gate - high - mid
            lane = lax.broadcasted_iota(jnp.int32, (step, 128), 1)
            tail = jnp.where(lane == 0, high, jnp.where(lane == 1, mid, jnp.where(lane == 2, low, 0.0)))
            out[at, hid:] = tail.astype(BF)
            return carry

        lax.fori_loop(0, rows // step, body, 0)

    return pl.pallas_call(
        kernel,
        grid=(1,),
        out_shape=jax.ShapeDtypeStruct((rows, hid + 128), BF),
        in_specs=[
            pl.BlockSpec((1, rows, hid), lambda n: (2, 0, 0)),
            pl.BlockSpec((1, rows, hid), lambda n: (2, 0, 0)),
            pl.BlockSpec((1, rows, hid), lambda n: (0, 0, 0)),
            pl.BlockSpec((rows, hid), lambda n: (0, 0)),
            pl.BlockSpec((rows, hid), lambda n: (0, 0)),
        ],
        out_specs=pl.BlockSpec((rows, hid + 128), lambda n: (0, 0)),
        cost_estimate=pl.CostEstimate(flops=3_000_000, bytes_accessed=3_000_000, transcendentals=200_000),
        name="grad_share",
    )(keep, got, near, last, pre)


def ranks_before(chosen):
    count = chosen.shape[-1]
    earlier = lax.broadcasted_iota(jnp.int32, (count, count), 0)
    later = lax.broadcasted_iota(jnp.int32, (count, count), 1)
    strict = (earlier < later).astype(BF)
    return jnp.dot(chosen.astype(BF), strict, preferred_element_type=F32)


def per_device(tokens, cotangent, expert_ids, gates, up_weight, down_weight):
    tok, width = tokens.shape
    top = expert_ids.shape[1]
    experts = NZ * NX
    cap = tok * top * 5 // (4 * experts)
    slots = experts * cap
    y, core = lax.axis_index("y"), lax.axis_index("core")
    w_up, w_down = up_weight[0], down_weight[0]
    hid = w_up.shape[1]

    side_y = 1 - 2 * ((y + core) % 2)
    turn = (jnp.arange(NY, dtype=jnp.int32) - y) % NY

    def share_at(side, places):
        near = jnp.where(turn == side % NY, places[1], places[2])
        return jnp.where(turn == 0, places[0], jnp.where(turn == 2, places[3], near))

    def gathered(side):
        return (y + jnp.stack([0 * side, side, -side, 0 * side + 2])) % NY

    table = jnp.concatenate([
        share_at(side_y, (2, 0, 3, 1)),
        share_at(-side_y, (2, 0, 3, 1)),
        gathered(side_y),
        gathered(-side_y),
        core[None],
    ]).astype(jnp.int32)

    ids_t, gates_t = expert_ids.T, gates.T
    routing = pl.BlockSpec((slots // 4, tok), lambda k: (k, 0))
    pick, gate_hi, gate_lo = pl.pallas_call(
        route_kernel,
        grid=(4,),
        out_shape=[jax.ShapeDtypeStruct((slots, tok), BF)] * 3,
        in_specs=[pl.BlockSpec((top, tok), lambda k: (0, 0))] * 2,
        out_specs=[routing] * 3,
        name="route",
    )(ids_t, gates_t)

    def reduce(slot_rows, weight, contract, ahead=()):
        keep, away = partial_sums(table, slot_rows, weight, contract)
        got = swap_core(away)
        send = (keep[:2] + got[:2].astype(F32)).astype(BF)
        near = swap(tie(send, *ahead) if ahead else send, 0)
        send = (keep[3] + got[3].astype(F32) + near[1].astype(F32)).astype(BF)
        return keep, got, near, swap(send, 1)

    def spread(share):
        pair = jnp.stack([share, swap(share, 0)])
        far = swap(pair, 1)
        return [pair, far, swap_core(pair), swap_core(far)]

    x_slots = scatter(select_rows(pick, (), tokens))
    g_slots = scatter(tie(select_rows(pick, (gate_hi, gate_lo), cotangent), x_slots))

    keep, got, near, last = reduce(x_slots, w_up, 0)
    pre = keep[2] + got[2].astype(F32) + near[0].astype(F32) + last.astype(F32)
    logistic = jax.nn.sigmoid(pre)
    hidden_part = (pre * logistic).astype(BF)
    out_rows, hidden = expand_rows(table, spread(hidden_part), w_down, 0)
    out_back = scatter(tie(out_rows, g_slots))

    keep, got, near, last = reduce(g_slots, w_down, 1)
    grads = spread(grad_share(keep, got, near, last, pre))
    dx_rows, pre_grad = expand_rows(table, grads, w_up, 1)
    dx_back = scatter(tie(dx_rows, out_back))

    mixed = mix_rows((gate_hi, gate_lo), out_back)
    down_grad = weight_grads(tie(hidden, dx_rows), g_slots, 256, "down_grads")
    up_grad = weight_grads(x_slots, pre_grad, 128, "up_grads")
    input_grads = mix_rows((pick,), tie(dx_back, down_grad, up_grad, mixed))

    zero_core = core == 0

    def slot_values(pair):
        return jnp.sum(pair[:, :, hid : hid + 3].astype(F32), axis=2)

    ring = jnp.concatenate([slot_values(grads[0]), slot_values(grads[1])])
    away = jnp.concatenate([slot_values(grads[2]), slot_values(grads[3])])

    def by_turn(value, side):
        up = side == 1
        return jnp.stack([value[0], jnp.where(up, value[1], value[2]), value[3],
                          jnp.where(up, value[2], value[1])])

    ring, away = by_turn(ring, side_y), by_turn(away, -side_y)
    ring = jnp.stack([jnp.where(zero_core, ring, away), jnp.where(zero_core, away, ring)], axis=1)
    gg = jnp.roll(ring, y, axis=0).reshape(experts, cap)
    gg = lax.all_to_all(gg, ("z", "x"), split_axis=0, concat_axis=0, tiled=True)
    own = ids_t[:, None, :] == jnp.arange(experts, dtype=jnp.int32)[None, :, None]
    token_hit = own.any(axis=0)
    token_place = jnp.where(token_hit, ranks_before(token_hit), -1.0)
    at = token_place[:, None, :] == jnp.arange(cap, dtype=F32)[None, :, None]
    value = jnp.sum(jnp.where(at, gg[:, :, None], 0.0), axis=1)
    gate_grads = (jnp.sum(jnp.where(own, value[None], 0.0), axis=1) / gates_t).T
    return mixed, input_grads, up_grad[None], down_grad[None], gate_grads


def solution(mesh):
    grid = Mesh(mesh.devices.reshape(NY, 2, NZ, NX), ("y", "core", "z", "x"))
    dp, ex = ("y", "core"), ("z", "x")
    return jax.shard_map(
        per_device,
        mesh=grid,
        in_specs=(P(ex, dp), P(ex, dp), P(ex, None), P(ex, None), P(ex, dp, None), P(ex, None, dp)),
        out_specs=(P(ex, dp), P(ex, dp), P(ex, dp, None), P(ex, None, dp), P(ex, None)),
        check_vma=False,
    )
```

```python
import jax
import jax.numpy as jnp
from jax import lax
from jax.experimental import pallas as pl
from jax.experimental.pallas import tpu as pltpu
from jax.sharding import Mesh
from jax.sharding import PartitionSpec as P

BF = jnp.bfloat16
F32 = jnp.float32

NZ, NX, NY = 8, 4, 4
CHUNKS = 4


ANY = pl.BlockSpec(memory_space=pl.ANY)
VMEM = pl.BlockSpec(memory_space=pltpu.VMEM)
SMEM = pl.BlockSpec(memory_space=pltpu.SMEM)


def swap(value, turn, apart=True):
    pairs = []
    for c in range(2):
        for i in range(NY):
            side = 1 if (i + (c if apart else 0) + turn) % 2 == 0 else -1
            pairs.append((2 * i + c, 2 * ((i + side) % NY) + c))
    return lax.ppermute(value, ("y", "core"), pairs)


def swap_core(value):
    return lax.ppermute(value, "core", [(0, 1), (1, 0)])


def tie(value, *others):
    return lax.optimization_barrier((value, *others))[0]


def scatter(rows):
    parts = rows.reshape(NZ * NX, rows.shape[0] // (NZ * NX), rows.shape[1])
    parts = lax.all_to_all(parts, ("z", "x"), split_axis=0, concat_axis=0, tiled=True)
    return parts.reshape(rows.shape)


def select_rows(pick, weights, values):
    slots, tok = pick.shape
    width = values.shape[1]
    step = slots // CHUNKS

    def kernel(pick_ref, *refs):
        weight_refs, (values_ref, out) = refs[: len(weights)], refs[len(weights) :]
        rows = jnp.dot(pick_ref[...], values_ref[...], preferred_element_type=F32)
        if weights:
            rows = rows * sum(
                jnp.sum(w[...].astype(F32), axis=1, keepdims=True) for w in weight_refs
            )
        out[...] = rows.astype(BF)

    chunk = pl.BlockSpec((step, tok), lambda k: (k, 0))
    return pl.pallas_call(
        kernel,
        grid=(CHUNKS,),
        out_shape=jax.ShapeDtypeStruct((slots, width), BF),
        in_specs=[chunk] * (1 + len(weights)) + [pl.BlockSpec((tok, width), lambda k: (0, 0))],
        out_specs=pl.BlockSpec((step, width), lambda k: (k, 0)),
        cost_estimate=pl.CostEstimate(flops=300_000_000, bytes_accessed=3_000_000, transcendentals=0),
        name="select_scaled" if weights else "select_plain",
    )(pick, *weights, values)


def mix_rows(picks, rows):
    slots, tok = picks[0].shape
    width = rows.shape[1]
    step = slots // CHUNKS

    def kernel(*refs):
        pick_refs, (rows_ref, out, total) = refs[: len(picks)], refs[len(picks) :]
        k = pl.program_id(0)
        part = None
        for ref in pick_refs:
            more = lax.dot_general(
                ref[...], rows_ref[...], (((0,), (0,)), ((), ())), preferred_element_type=F32
            )
            part = more if part is None else part + more

        @pl.when(k == 0)
        def _():
            total[...] = part

        @pl.when(k > 0)
        def _():
            total[...] += part

        @pl.when(k == CHUNKS - 1)
        def _():
            out[...] = total[...].astype(BF)

    return pl.pallas_call(
        kernel,
        grid=(CHUNKS,),
        out_shape=jax.ShapeDtypeStruct((tok, width), BF),
        in_specs=[pl.BlockSpec((step, tok), lambda k: (k, 0))] * len(picks)
        + [pl.BlockSpec((step, width), lambda k: (k, 0))],
        out_specs=pl.BlockSpec((tok, width), lambda k: (0, 0)),
        scratch_shapes=[pltpu.VMEM((tok, width), F32)],
        cost_estimate=pl.CostEstimate(
            flops=300_000_000 * len(picks), bytes_accessed=3_000_000, transcendentals=0
        ),
    )(*picks, rows)


def gate_terms(pick, rows, values):
    slots, tok = pick.shape
    width = rows.shape[1]
    step = slots // CHUNKS
    each = NZ * NX // CHUNKS
    cap = step // each

    def kernel(pick_ref, rows_ref, values_ref, out):
        chosen = jnp.dot(pick_ref[...], values_ref[...], preferred_element_type=F32)
        term = jnp.sum(chosen * rows_ref[...].astype(F32), axis=1, keepdims=True)
        placed = pick_ref[...].astype(F32) * term
        out[...] = jnp.concatenate(
            [
                jnp.sum(placed[n * cap : (n + 1) * cap], axis=0, keepdims=True)
                for n in range(each)
            ],
            axis=0,
        )

    return pl.pallas_call(
        kernel,
        grid=(CHUNKS,),
        out_shape=jax.ShapeDtypeStruct((NZ * NX, tok), F32),
        in_specs=[
            pl.BlockSpec((step, tok), lambda k: (k, 0)),
            pl.BlockSpec((step, width), lambda k: (k, 0)),
            pl.BlockSpec((tok, width), lambda k: (0, 0)),
        ],
        out_specs=pl.BlockSpec((each, tok), lambda k: (k, 0)),
        cost_estimate=pl.CostEstimate(flops=300_000_000, bytes_accessed=3_000_000, transcendentals=0),
        name="gate_terms",
    )(pick, rows, values)


def partial_sums(table, slot_rows, weight, contract):
    slots, width = slot_rows.shape
    rows = slots // (2 * NY)
    hid = weight.shape[1 - contract]
    step = 256

    def kernel(table_ref, weight_ref, rows_ref, keep, away, held, sems):
        first = pl.program_id(0) == 0
        core = table_ref[4 * NY]

        def get(i, h):
            return pltpu.make_async_copy(
                rows_ref.at[i, h ^ core], held.at[pl.ds((2 * i + h) * rows, rows)], sems.at[i, h]
            )

        @pl.when(first)
        def _():
            for i in range(NY):
                for h in range(2):
                    get(i, h).start()

        for i in range(NY):
            at = i * 2 * rows

            @pl.when(first)
            def _():
                for h in range(2):
                    get(i, h).wait()

            made = lax.dot_general(
                held[at : at + 2 * rows], weight_ref[...], (((1,), (contract,)), ((), ())),
                preferred_element_type=F32,
            )
            keep[table_ref[i]] = made[:rows]
            away[table_ref[NY + i]] = made[rows:].astype(BF)

    if contract == 0:
        weight_spec = pl.BlockSpec((width, step), lambda n: (0, n))
    else:
        weight_spec = pl.BlockSpec((step, width), lambda n: (n, 0))
    out_spec = pl.BlockSpec((NY, rows, step), lambda n: (0, 0, n))
    return pl.pallas_call(
        kernel,
        grid=(hid // step,),
        out_shape=[
            jax.ShapeDtypeStruct((NY, rows, hid), F32), jax.ShapeDtypeStruct((NY, rows, hid), BF)
        ],
        in_specs=[SMEM, weight_spec, ANY],
        out_specs=[out_spec] * 2,
        scratch_shapes=[pltpu.VMEM((slots, width), BF), pltpu.SemaphoreType.DMA((NY, 2))],
        cost_estimate=pl.CostEstimate(
            flops=2_400_000_000, bytes_accessed=9_000_000, transcendentals=0
        ),
    )(table, weight, slot_rows.reshape(NY, 2, rows, width))


def expand_rows(table, shares, weight, contract):
    rows = shares[0].shape[1]
    hid, width = weight.shape[contract], weight.shape[1 - contract]

    def kernel(table_ref, weight_ref, *refs):
        ins, (out, joined, held, made, held_weight, in_sems, out_sems, join_sems, weight_sem) = (
            refs[:4], refs[4:]
        )
        core = table_ref[4 * NY]
        fetch = pltpu.make_async_copy(weight_ref, held_weight, weight_sem)
        fetch.start()
        for n in range(4):
            for m in range(2):
                place = table_ref[2 * NY + 2 * n + m]
                half = core if n < 2 else 1 - core
                pltpu.make_async_copy(
                    ins[n].at[m], held.at[place, half], in_sems.at[place, half]
                ).start()

        def put(i):
            return pltpu.make_async_copy(made.at[i], out.at[i], out_sems.at[i])

        def keep(i):
            return pltpu.make_async_copy(held.at[i], joined.at[i], join_sems.at[i])

        fetch.wait()

        def step(i, carry):
            for h in range(2):
                pltpu.make_async_copy(ins[0].at[0], held.at[i, h], in_sems.at[i, h]).wait()
            keep(i).start()
            made[i] = lax.dot_general(
                held[i].reshape(2 * rows, hid), held_weight[...],
                (((1,), (contract,)), ((), ())), preferred_element_type=F32,
            ).astype(BF)
            put(i).start()
            return carry

        lax.fori_loop(0, NY, step, 0)
        for i in range(NY):
            put(i).wait()
            keep(i).wait()

    out, joined = pl.pallas_call(
        kernel,
        out_shape=[
            jax.ShapeDtypeStruct((NY, 2 * rows, width), BF),
            jax.ShapeDtypeStruct((NY, 2, rows, hid), BF),
        ],
        in_specs=[SMEM, ANY] + [ANY] * 4,
        out_specs=[ANY] * 2,
        scratch_shapes=[
            pltpu.VMEM((NY, 2, rows, hid), BF),
            pltpu.VMEM((NY, 2 * rows, width), BF),
            pltpu.VMEM(weight.shape, BF),
            pltpu.SemaphoreType.DMA((NY, 2)),
            pltpu.SemaphoreType.DMA((NY,)),
            pltpu.SemaphoreType.DMA((NY,)),
            pltpu.SemaphoreType.DMA,
        ],
        cost_estimate=pl.CostEstimate(
            flops=2_400_000_000, bytes_accessed=9_000_000, transcendentals=0
        ),
    )(table, weight, *shares)
    return out.reshape(NY * 2 * rows, width), joined.reshape(NY * 2 * rows, hid)


def weight_grads(left, right, step):
    slots, count = left.shape
    width = right.shape[1]

    def kernel(left_ref, right_ref, out):
        out[...] = lax.dot_general(
            left_ref[...], right_ref[...], (((0,), (0,)), ((), ())), preferred_element_type=F32
        ).astype(BF)

    return pl.pallas_call(
        kernel,
        grid=(count // step,),
        out_shape=jax.ShapeDtypeStruct((count, width), BF),
        in_specs=[
            pl.BlockSpec((slots, step), lambda n: (0, n)),
            pl.BlockSpec((slots, width), lambda n: (0, 0)),
        ],
        out_specs=pl.BlockSpec((step, width), lambda n: (n, 0)),
        cost_estimate=pl.CostEstimate(
            flops=2_400_000_000, bytes_accessed=7_000_000, transcendentals=0
        ),
    )(left, right)


def route_kernel(ids_ref, gates_ref, tokens_ref, pick_ref, hi_ref, lo_ref, rows_ref):
    tok = ids_ref.shape[1]
    each = 8
    cap = pick_ref.shape[0] // each
    chosen, weight = [], []
    for n in range(each):
        hit = jnp.where(ids_ref[...] == pl.program_id(0) * each + n, 1.0, 0.0)
        chosen.append(jnp.sum(hit, axis=0, keepdims=True))
        weight.append(jnp.sum(hit * gates_ref[...], axis=0, keepdims=True))
    chosen = jnp.concatenate(chosen, axis=0)
    earlier = lax.broadcasted_iota(jnp.int32, (tok, tok), 0)
    later = lax.broadcasted_iota(jnp.int32, (tok, tok), 1)
    strict = jnp.where(earlier < later, 1.0, 0.0).astype(BF)
    rank = jnp.dot(chosen.astype(BF), strict, preferred_element_type=F32)
    place = jnp.where(chosen > 0.0, rank, -1.0)
    slot = lax.broadcasted_iota(jnp.int32, (cap, tok), 0).astype(F32)
    one, high, low = [], [], []
    for n in range(each):
        here = slot == place[n : n + 1]
        gate = jnp.where(here, jnp.broadcast_to(weight[n], (cap, tok)), 0.0)
        one.append(jnp.where(here, 1.0, 0.0))
        high.append(gate.astype(BF).astype(F32))
        low.append(gate - high[-1])
    pick = jnp.concatenate(one, axis=0).astype(BF)
    pick_ref[...] = pick
    rows_ref[...] = jnp.dot(pick, tokens_ref[...], preferred_element_type=F32).astype(BF)
    hi_ref[...] = jnp.concatenate(high, axis=0).astype(BF)
    lo_ref[...] = jnp.concatenate(low, axis=0).astype(BF)


def grad_share(keep, got, near, last, pre):
    rows, hid = pre.shape
    step = 16

    def kernel(keep_ref, got_ref, near_ref, last_ref, pre_ref, out):
        def body(n, carry):
            at = pl.ds(pl.multiple_of(n * step, step), step)
            raw = keep_ref[0, at].astype(F32) + got_ref[0, at].astype(F32)
            raw = raw + near_ref[0, at].astype(F32) + last_ref[at].astype(F32)
            pre = pre_ref[at]
            logistic = 1.0 / (1.0 + jnp.exp(-pre))
            out[at] = (raw * (logistic * (1.0 + pre * (1.0 - logistic)))).astype(BF)
            return carry

        lax.fori_loop(0, rows // step, body, 0)

    return pl.pallas_call(
        kernel,
        grid=(1,),
        out_shape=jax.ShapeDtypeStruct((rows, hid), BF),
        in_specs=[
            pl.BlockSpec((1, rows, hid), lambda n: (2, 0, 0)),
            pl.BlockSpec((1, rows, hid), lambda n: (2, 0, 0)),
            pl.BlockSpec((1, rows, hid), lambda n: (0, 0, 0)),
            pl.BlockSpec((rows, hid), lambda n: (0, 0)),
            pl.BlockSpec((rows, hid), lambda n: (0, 0)),
        ],
        out_specs=pl.BlockSpec((rows, hid), lambda n: (0, 0)),
        cost_estimate=pl.CostEstimate(flops=3_000_000, bytes_accessed=3_000_000, transcendentals=200_000),
        name="grad_share",
    )(keep, got, near, last, pre)


def per_device(tokens, cotangent, expert_ids, gates, up_weight, down_weight):
    tok, width = tokens.shape
    top = expert_ids.shape[1]
    experts = NZ * NX
    cap = tok * top * 5 // (4 * experts)
    slots = experts * cap
    y, core = lax.axis_index("y"), lax.axis_index("core")
    w_up, w_down = up_weight[0], down_weight[0]

    side_y = 1 - 2 * ((y + core) % 2)
    turn = (jnp.arange(NY, dtype=jnp.int32) - y) % NY

    def share_at(side, places):
        near = jnp.where(turn == side % NY, places[1], places[2])
        return jnp.where(turn == 0, places[0], jnp.where(turn == 2, places[3], near))

    def gathered(side):
        return (y + jnp.stack([0 * side, side, -side, 0 * side + 2])) % NY

    table = jnp.concatenate([
        share_at(side_y, (2, 0, 3, 1)),
        share_at(-side_y, (2, 0, 3, 1)),
        gathered(side_y),
        gathered(-side_y),
        core[None],
    ]).astype(jnp.int32)

    ids_t, gates_t = expert_ids.T, gates.T
    routing = pl.BlockSpec((slots // 4, tok), lambda k: (k, 0))
    small = pl.BlockSpec((top, tok), lambda k: (0, 0))
    pick, gate_hi, gate_lo, x_rows = pl.pallas_call(
        route_kernel,
        grid=(4,),
        out_shape=[jax.ShapeDtypeStruct((slots, tok), BF)] * 3
        + [jax.ShapeDtypeStruct((slots, width), BF)],
        in_specs=[small, small, pl.BlockSpec((tok, width), lambda k: (0, 0))],
        out_specs=[routing] * 3 + [pl.BlockSpec((slots // 4, width), lambda k: (k, 0))],
        name="route",
    )(ids_t, gates_t, tokens)

    def reduce(keep, away):
        got = swap_core(away)
        first = (keep[:2] + got[:2].astype(F32)).astype(BF)
        near = swap(first, 0)
        second = (keep[3] + got[3].astype(F32) + near[1].astype(F32)).astype(BF)
        return got, near, swap(second, 1), first

    def spread(share):
        pair = jnp.stack([share, swap(share, 0)])
        other_pair = swap_core(pair)
        far = swap(pair, 1)
        other_far = swap_core(far)
        return [pair, far, other_pair, other_far]

    x_slots = scatter(x_rows)
    g_slots = scatter(tie(select_rows(pick, (gate_hi, gate_lo), cotangent), x_slots))

    keep, away = partial_sums(table, x_slots, w_up, 0)
    got, near, last, _ = reduce(keep, away)
    pre = keep[2] + got[2].astype(F32) + near[0].astype(F32) + last.astype(F32)
    hidden_shares = spread((pre * jax.nn.sigmoid(pre)).astype(BF))

    keep, away = partial_sums(table, tie(g_slots, hidden_shares[1]), w_down, 1)
    got, near, last, first = reduce(keep, away)
    hidden_shares[0] = tie(hidden_shares[0], keep)
    out_rows, hidden = expand_rows(table, hidden_shares, w_down, 0)
    out_back = scatter(tie(out_rows, first))

    grads = spread(grad_share(keep, got, near, last, pre))
    dx_rows, pre_grad = expand_rows(table, grads, w_up, 1)
    dx_back = scatter(tie(dx_rows, out_back))

    mixed = mix_rows((gate_hi, gate_lo), out_back)
    terms = gate_terms(pick, tie(out_back, dx_rows), cotangent)
    terms = terms + swap_core(terms)
    terms = terms + swap(terms, 0, False)
    terms = terms + swap(terms, 1, False)
    own = ids_t[:, None, :] == jnp.arange(experts, dtype=jnp.int32)[None, :, None]
    gate_grads = jnp.sum(jnp.where(own, terms[None], 0.0), axis=1).T
    down_grad = weight_grads(tie(hidden, dx_rows), g_slots, 256)
    up_grad = weight_grads(x_slots, pre_grad, 128)
    input_grads = mix_rows((pick,), tie(dx_back, down_grad, up_grad, mixed))
    return mixed, input_grads, up_grad[None], down_grad[None], gate_grads


def solution(mesh):
    grid = Mesh(mesh.devices.reshape(NY, 2, NZ, NX), ("y", "core", "z", "x"))
    dp, ex = ("y", "core"), ("z", "x")
    return jax.shard_map(
        per_device,
        mesh=grid,
        in_specs=(P(ex, dp), P(ex, dp), P(ex, None), P(ex, None), P(ex, dp, None), P(ex, None, dp)),
        out_specs=(P(ex, dp), P(ex, dp), P(ex, dp, None), P(ex, None, dp), P(ex, None)),
        check_vma=False,
    )
```

```python
import jax
import jax.numpy as jnp
from jax import lax
from jax.experimental import pallas as pl
from jax.experimental.pallas import tpu as pltpu
from jax.sharding import Mesh
from jax.sharding import PartitionSpec as P

BF = jnp.bfloat16
F32 = jnp.float32

NZ, NX, NY = 8, 4, 4
CHUNKS = 4


ANY = pl.BlockSpec(memory_space=pl.ANY)
VMEM = pl.BlockSpec(memory_space=pltpu.VMEM)
SMEM = pl.BlockSpec(memory_space=pltpu.SMEM)


def swap(value, turn, apart=True):
    pairs = []
    for c in range(2):
        for i in range(NY):
            side = 1 if (i + (c if apart else 0) + turn) % 2 == 0 else -1
            pairs.append((2 * i + c, 2 * ((i + side) % NY) + c))
    return lax.ppermute(value, ("y", "core"), pairs)


def swap_core(value):
    return lax.ppermute(value, "core", [(0, 1), (1, 0)])


def tie(value, *others):
    return lax.optimization_barrier((value, *others))[0]


def scatter(rows):
    parts = rows.reshape(NZ * NX, rows.shape[0] // (NZ * NX), rows.shape[1])
    parts = lax.all_to_all(parts, ("z", "x"), split_axis=0, concat_axis=0, tiled=True)
    return parts.reshape(rows.shape)


def select_rows(pick, weights, values):
    slots, tok = pick.shape
    width = values.shape[1]
    step = slots // CHUNKS

    def kernel(pick_ref, *refs):
        weight_refs, (values_ref, out) = refs[: len(weights)], refs[len(weights) :]
        rows = jnp.dot(pick_ref[...], values_ref[...], preferred_element_type=F32)
        if weights:
            rows = rows * sum(
                jnp.sum(w[...].astype(F32), axis=1, keepdims=True) for w in weight_refs
            )
        out[...] = rows.astype(BF)

    chunk = pl.BlockSpec((step, tok), lambda k: (k, 0))
    return pl.pallas_call(
        kernel,
        grid=(CHUNKS,),
        out_shape=jax.ShapeDtypeStruct((slots, width), BF),
        in_specs=[chunk] * (1 + len(weights)) + [pl.BlockSpec((tok, width), lambda k: (0, 0))],
        out_specs=pl.BlockSpec((step, width), lambda k: (k, 0)),
        cost_estimate=pl.CostEstimate(flops=300_000_000, bytes_accessed=3_000_000, transcendentals=0),
        name="select_scaled" if weights else "select_plain",
    )(pick, *weights, values)


def mix_rows(picks, rows):
    tok, slots = picks[0].shape
    width = rows.shape[1]
    count = 2
    step = slots // count

    def kernel(*refs):
        pick_refs, (rows_ref, out, total) = refs[: len(picks)], refs[len(picks) :]
        k = pl.program_id(0)
        part = None
        for ref in pick_refs:
            more = jnp.dot(ref[...], rows_ref[...], preferred_element_type=F32)
            part = more if part is None else part + more

        @pl.when(k == 0)
        def _():
            total[...] = part

        @pl.when(k > 0)
        def _():
            total[...] += part

        @pl.when(k == count - 1)
        def _():
            out[...] = total[...].astype(BF)

    return pl.pallas_call(
        kernel,
        grid=(count,),
        out_shape=jax.ShapeDtypeStruct((tok, width), BF),
        in_specs=[pl.BlockSpec((tok, step), lambda k: (0, k))] * len(picks)
        + [pl.BlockSpec((step, width), lambda k: (k, 0))],
        out_specs=pl.BlockSpec((tok, width), lambda k: (0, 0)),
        scratch_shapes=[pltpu.VMEM((tok, width), F32)],
        cost_estimate=pl.CostEstimate(
            flops=300_000_000 * len(picks), bytes_accessed=3_000_000, transcendentals=0
        ),
    )(*picks, rows)


def gate_terms(pick, rows, values):
    slots, tok = pick.shape
    width = rows.shape[1]
    step = slots // CHUNKS
    each = NZ * NX // CHUNKS
    cap = step // each

    def kernel(pick_ref, rows_ref, values_ref, out):
        chosen = jnp.dot(pick_ref[...], values_ref[...], preferred_element_type=F32)
        term = jnp.sum(chosen * rows_ref[...].astype(F32), axis=1, keepdims=True)
        placed = pick_ref[...].astype(F32) * term
        out[...] = jnp.concatenate(
            [
                jnp.sum(placed[n * cap : (n + 1) * cap], axis=0, keepdims=True)
                for n in range(each)
            ],
            axis=0,
        )

    return pl.pallas_call(
        kernel,
        grid=(CHUNKS,),
        out_shape=jax.ShapeDtypeStruct((NZ * NX, tok), F32),
        in_specs=[
            pl.BlockSpec((step, tok), lambda k: (k, 0)),
            pl.BlockSpec((step, width), lambda k: (k, 0)),
            pl.BlockSpec((tok, width), lambda k: (0, 0)),
        ],
        out_specs=pl.BlockSpec((each, tok), lambda k: (k, 0)),
        cost_estimate=pl.CostEstimate(flops=300_000_000, bytes_accessed=3_000_000, transcendentals=0),
        name="gate_terms",
    )(pick, rows, values)


def partial_sums(table, slot_rows, weight, contract):
    slots, width = slot_rows.shape
    rows = slots // (2 * NY)
    hid = weight.shape[1 - contract]
    step = 256

    def kernel(table_ref, weight_ref, rows_ref, keep, away, held, sems):
        @pl.when(pl.program_id(0) == 0)
        def _():
            core = table_ref[4 * NY]
            copies = [
                pltpu.make_async_copy(
                    rows_ref.at[i, h ^ core], held.at[pl.ds((2 * i + h) * rows, rows)], sems.at[i, h]
                )
                for i in range(NY)
                for h in range(2)
            ]
            for c in copies:
                c.start()
            for c in copies:
                c.wait()

        made = lax.dot_general(
            held[...], weight_ref[...], (((1,), (contract,)), ((), ())),
            preferred_element_type=F32,
        )
        for i in range(NY):
            at = i * 2 * rows
            keep[table_ref[i]] = made[at : at + rows]
            away[table_ref[NY + i]] = made[at + rows : at + 2 * rows].astype(BF)

    if contract == 0:
        weight_spec = pl.BlockSpec((width, step), lambda n: (0, n))
    else:
        weight_spec = pl.BlockSpec((step, width), lambda n: (n, 0))
    out_spec = pl.BlockSpec((NY, rows, step), lambda n: (0, 0, n))
    return pl.pallas_call(
        kernel,
        grid=(hid // step,),
        out_shape=[
            jax.ShapeDtypeStruct((NY, rows, hid), F32), jax.ShapeDtypeStruct((NY, rows, hid), BF)
        ],
        in_specs=[SMEM, weight_spec, ANY],
        out_specs=[out_spec] * 2,
        scratch_shapes=[pltpu.VMEM((slots, width), BF), pltpu.SemaphoreType.DMA((NY, 2))],
        cost_estimate=pl.CostEstimate(
            flops=2_400_000_000, bytes_accessed=9_000_000, transcendentals=0
        ),
    )(table, weight, slot_rows.reshape(NY, 2, rows, width))


def expand_rows(table, shares, weight, contract):
    rows = shares[0].shape[1]
    hid, width = weight.shape[contract], weight.shape[1 - contract]

    def kernel(table_ref, weight_ref, *refs):
        ins, (out, joined, held, made, held_weight, in_sems, out_sems, join_sems, weight_sem) = (
            refs[:4], refs[4:]
        )
        core = table_ref[4 * NY]
        fetch = pltpu.make_async_copy(weight_ref, held_weight, weight_sem)
        fetch.start()
        for n in range(4):
            for m in range(2):
                place = table_ref[2 * NY + 2 * n + m]
                half = core if n < 2 else 1 - core
                pltpu.make_async_copy(
                    ins[n].at[m], held.at[place, half], in_sems.at[place, half]
                ).start()

        def put(i):
            return pltpu.make_async_copy(made.at[i], out.at[i], out_sems.at[i])

        def keep(i):
            return pltpu.make_async_copy(held.at[i], joined.at[i], join_sems.at[i])

        fetch.wait()

        def step(i, carry):
            for h in range(2):
                pltpu.make_async_copy(ins[0].at[0], held.at[i, h], in_sems.at[i, h]).wait()
            keep(i).start()
            made[i] = lax.dot_general(
                held[i].reshape(2 * rows, hid), held_weight[...],
                (((1,), (contract,)), ((), ())), preferred_element_type=F32,
            ).astype(BF)
            put(i).start()
            return carry

        lax.fori_loop(0, NY, step, 0)
        for i in range(NY):
            put(i).wait()
            keep(i).wait()

    out, joined = pl.pallas_call(
        kernel,
        out_shape=[
            jax.ShapeDtypeStruct((NY, 2 * rows, width), BF),
            jax.ShapeDtypeStruct((NY, 2, rows, hid), BF),
        ],
        in_specs=[SMEM, ANY] + [ANY] * 4,
        out_specs=[ANY] * 2,
        scratch_shapes=[
            pltpu.VMEM((NY, 2, rows, hid), BF),
            pltpu.VMEM((NY, 2 * rows, width), BF),
            pltpu.VMEM(weight.shape, BF),
            pltpu.SemaphoreType.DMA((NY, 2)),
            pltpu.SemaphoreType.DMA((NY,)),
            pltpu.SemaphoreType.DMA((NY,)),
            pltpu.SemaphoreType.DMA,
        ],
        cost_estimate=pl.CostEstimate(
            flops=2_400_000_000, bytes_accessed=9_000_000, transcendentals=0
        ),
    )(table, weight, *shares)
    return out.reshape(NY * 2 * rows, width), joined.reshape(NY * 2 * rows, hid)


def weight_grads(left, right, step):
    slots, count = left.shape
    width = right.shape[1]

    def kernel(left_ref, right_ref, out):
        out[...] = lax.dot_general(
            left_ref[...], right_ref[...], (((0,), (0,)), ((), ())), preferred_element_type=F32
        ).astype(BF)

    return pl.pallas_call(
        kernel,
        grid=(count // step,),
        out_shape=jax.ShapeDtypeStruct((count, width), BF),
        in_specs=[
            pl.BlockSpec((slots, step), lambda n: (0, n)),
            pl.BlockSpec((slots, width), lambda n: (0, 0)),
        ],
        out_specs=pl.BlockSpec((step, width), lambda n: (n, 0)),
        cost_estimate=pl.CostEstimate(
            flops=2_400_000_000, bytes_accessed=7_000_000, transcendentals=0
        ),
    )(left, right)


def route_kernel(ids_ref, gates_ref, tokens_ref, pick_ref, hi_ref, lo_ref, rows_ref):
    tok = ids_ref.shape[1]
    each = 8
    cap = pick_ref.shape[0] // each
    chosen, weight = [], []
    for n in range(each):
        hit = jnp.where(ids_ref[...] == pl.program_id(0) * each + n, 1.0, 0.0)
        chosen.append(jnp.sum(hit, axis=0, keepdims=True))
        weight.append(jnp.sum(hit * gates_ref[...], axis=0, keepdims=True))
    chosen = jnp.concatenate(chosen, axis=0)
    earlier = lax.broadcasted_iota(jnp.int32, (tok, tok), 0)
    later = lax.broadcasted_iota(jnp.int32, (tok, tok), 1)
    strict = jnp.where(earlier < later, 1.0, 0.0).astype(BF)
    rank = jnp.dot(chosen.astype(BF), strict, preferred_element_type=F32)
    place = jnp.where(chosen > 0.0, rank, -1.0)
    slot = lax.broadcasted_iota(jnp.int32, (cap, tok), 0).astype(F32)
    one, high, low = [], [], []
    for n in range(each):
        here = slot == place[n : n + 1]
        gate = jnp.where(here, jnp.broadcast_to(weight[n], (cap, tok)), 0.0)
        one.append(jnp.where(here, 1.0, 0.0))
        high.append(gate.astype(BF).astype(F32))
        low.append(gate - high[-1])
    pick = jnp.concatenate(one, axis=0).astype(BF)
    pick_ref[...] = pick
    rows_ref[...] = jnp.dot(pick, tokens_ref[...], preferred_element_type=F32).astype(BF)
    hi_ref[...] = jnp.concatenate(high, axis=0).astype(BF)
    lo_ref[...] = jnp.concatenate(low, axis=0).astype(BF)


def grad_share(keep, got, near, last, pre):
    rows, hid = pre.shape
    step = 16

    def kernel(keep_ref, got_ref, near_ref, last_ref, pre_ref, out):
        def body(n, carry):
            at = pl.ds(pl.multiple_of(n * step, step), step)
            raw = keep_ref[0, at].astype(F32) + got_ref[0, at].astype(F32)
            raw = raw + near_ref[0, at].astype(F32) + last_ref[at].astype(F32)
            pre = pre_ref[at]
            logistic = 1.0 / (1.0 + jnp.exp(-pre))
            out[at] = (raw * (logistic * (1.0 + pre * (1.0 - logistic)))).astype(BF)
            return carry

        lax.fori_loop(0, rows // step, body, 0)

    return pl.pallas_call(
        kernel,
        grid=(1,),
        out_shape=jax.ShapeDtypeStruct((rows, hid), BF),
        in_specs=[
            pl.BlockSpec((1, rows, hid), lambda n: (2, 0, 0)),
            pl.BlockSpec((1, rows, hid), lambda n: (2, 0, 0)),
            pl.BlockSpec((1, rows, hid), lambda n: (0, 0, 0)),
            pl.BlockSpec((rows, hid), lambda n: (0, 0)),
            pl.BlockSpec((rows, hid), lambda n: (0, 0)),
        ],
        out_specs=pl.BlockSpec((rows, hid), lambda n: (0, 0)),
        cost_estimate=pl.CostEstimate(flops=3_000_000, bytes_accessed=3_000_000, transcendentals=200_000),
        name="grad_share",
    )(keep, got, near, last, pre)


def per_device(tokens, cotangent, expert_ids, gates, up_weight, down_weight):
    tok, width = tokens.shape
    top = expert_ids.shape[1]
    experts = NZ * NX
    cap = tok * top * 5 // (4 * experts)
    slots = experts * cap
    y, core = lax.axis_index("y"), lax.axis_index("core")
    w_up, w_down = up_weight[0], down_weight[0]

    side_y = 1 - 2 * ((y + core) % 2)
    turn = (jnp.arange(NY, dtype=jnp.int32) - y) % NY

    def share_at(side, places):
        near = jnp.where(turn == side % NY, places[1], places[2])
        return jnp.where(turn == 0, places[0], jnp.where(turn == 2, places[3], near))

    def gathered(side):
        return (y + jnp.stack([0 * side, side, -side, 0 * side + 2])) % NY

    table = jnp.concatenate([
        share_at(side_y, (2, 0, 3, 1)),
        share_at(-side_y, (2, 0, 3, 1)),
        gathered(side_y),
        gathered(-side_y),
        core[None],
    ]).astype(jnp.int32)

    ids_t, gates_t = expert_ids.T, gates.T
    routing = pl.BlockSpec((slots // 4, tok), lambda k: (k, 0))
    small = pl.BlockSpec((top, tok), lambda k: (0, 0))
    pick, gate_hi, gate_lo, x_rows = pl.pallas_call(
        route_kernel,
        grid=(4,),
        out_shape=[jax.ShapeDtypeStruct((slots, tok), BF)] * 3
        + [jax.ShapeDtypeStruct((slots, width), BF)],
        in_specs=[small, small, pl.BlockSpec((tok, width), lambda k: (0, 0))],
        out_specs=[routing] * 3 + [pl.BlockSpec((slots // 4, width), lambda k: (k, 0))],
        name="route",
    )(ids_t, gates_t, tokens)

    def reduce(keep, away):
        got = swap_core(away)
        first = (keep[:2] + got[:2].astype(F32)).astype(BF)
        near = swap(first, 0)
        second = (keep[3] + got[3].astype(F32) + near[1].astype(F32)).astype(BF)
        return got, near, swap(second, 1), first

    def spread(share):
        pair = jnp.stack([share, swap(share, 0)])
        other_pair = swap_core(pair)
        far = swap(pair, 1)
        other_far = swap_core(far)
        return [pair, far, other_pair, other_far]

    x_slots = scatter(x_rows)
    g_slots = scatter(tie(select_rows(pick, (gate_hi, gate_lo), cotangent), x_slots))

    keep, away = partial_sums(table, x_slots, w_up, 0)
    got, near, last, _ = reduce(keep, away)
    pre = keep[2] + got[2].astype(F32) + near[0].astype(F32) + last.astype(F32)
    hidden_shares = spread((pre * jax.nn.sigmoid(pre)).astype(BF))

    keep, away = partial_sums(table, tie(g_slots, hidden_shares[1]), w_down, 1)
    got, near, last, first = reduce(keep, away)
    hidden_shares[0] = tie(hidden_shares[0], keep)
    out_rows, hidden = expand_rows(table, hidden_shares, w_down, 0)
    out_back = scatter(tie(out_rows, first))

    grads = spread(grad_share(keep, got, near, last, pre))
    dx_rows, pre_grad = expand_rows(table, grads, w_up, 1)
    dx_back = scatter(tie(dx_rows, out_back))

    mixed = mix_rows((gate_hi.T, gate_lo.T), out_back)
    terms = gate_terms(pick, tie(out_back, dx_rows), cotangent)
    terms = terms + swap_core(terms)
    terms = terms + swap(terms, 0, False)
    terms = terms + swap(terms, 1, False)
    own = ids_t[:, None, :] == jnp.arange(experts, dtype=jnp.int32)[None, :, None]
    gate_grads = jnp.sum(jnp.where(own, terms[None], 0.0), axis=1).T
    down_grad = weight_grads(tie(hidden, dx_rows), g_slots, 256)
    up_grad = weight_grads(x_slots, pre_grad, 128)
    input_grads = mix_rows((pick.T,), tie(dx_back, down_grad, up_grad, mixed))
    return mixed, input_grads, up_grad[None], down_grad[None], gate_grads


def solution(mesh):
    grid = Mesh(mesh.devices.reshape(NY, 2, NZ, NX), ("y", "core", "z", "x"))
    dp, ex = ("y", "core"), ("z", "x")
    return jax.shard_map(
        per_device,
        mesh=grid,
        in_specs=(P(ex, dp), P(ex, dp), P(ex, None), P(ex, None), P(ex, dp, None), P(ex, None, dp)),
        out_specs=(P(ex, dp), P(ex, dp), P(ex, dp, None), P(ex, None, dp), P(ex, None)),
        check_vma=False,
    )
```

```python
import jax
import jax.numpy as jnp
from jax import lax
from jax.experimental import pallas as pl
from jax.experimental.pallas import tpu as pltpu
from jax.sharding import Mesh
from jax.sharding import PartitionSpec as P

BF = jnp.bfloat16
F32 = jnp.float32

NZ, NX, NY = 8, 4, 4
CHUNKS = 4


ANY = pl.BlockSpec(memory_space=pl.ANY)
VMEM = pl.BlockSpec(memory_space=pltpu.VMEM)
SMEM = pl.BlockSpec(memory_space=pltpu.SMEM)


def swap(value, turn, apart=True):
    pairs = []
    for c in range(2):
        for i in range(NY):
            side = 1 if (i + (c if apart else 0) + turn) % 2 == 0 else -1
            pairs.append((2 * i + c, 2 * ((i + side) % NY) + c))
    return lax.ppermute(value, ("y", "core"), pairs)


def swap_core(value):
    return lax.ppermute(value, "core", [(0, 1), (1, 0)])


def tie(value, *others):
    return lax.optimization_barrier((value, *others))[0]


def scatter(rows):
    parts = rows.reshape(NZ * NX, rows.shape[0] // (NZ * NX), rows.shape[1])
    parts = lax.all_to_all(parts, ("z", "x"), split_axis=0, concat_axis=0, tiled=True)
    return parts.reshape(rows.shape)


def select_rows(pick, weights, values):
    slots, tok = pick.shape
    width = values.shape[1]
    step = slots // CHUNKS

    def kernel(pick_ref, *refs):
        weight_refs, (values_ref, out) = refs[: len(weights)], refs[len(weights) :]
        rows = jnp.dot(pick_ref[...], values_ref[...], preferred_element_type=F32)
        if weights:
            rows = rows * sum(
                jnp.sum(w[...].astype(F32), axis=1, keepdims=True) for w in weight_refs
            )
        out[...] = rows.astype(BF)

    chunk = pl.BlockSpec((step, tok), lambda k: (k, 0))
    return pl.pallas_call(
        kernel,
        grid=(CHUNKS,),
        out_shape=jax.ShapeDtypeStruct((slots, width), BF),
        in_specs=[chunk] * (1 + len(weights)) + [pl.BlockSpec((tok, width), lambda k: (0, 0))],
        out_specs=pl.BlockSpec((step, width), lambda k: (k, 0)),
        cost_estimate=pl.CostEstimate(flops=300_000_000, bytes_accessed=3_000_000, transcendentals=0),
        name="select_scaled" if weights else "select_plain",
    )(pick, *weights, values)


def mix_rows(picks, rows):
    tok, slots = picks[0].shape
    width = rows.shape[1]
    count = 2
    step = slots // count

    def kernel(*refs):
        pick_refs, (rows_ref, out, total) = refs[: len(picks)], refs[len(picks) :]
        k = pl.program_id(0)
        part = None
        for ref in pick_refs:
            more = jnp.dot(ref[...], rows_ref[...], preferred_element_type=F32)
            part = more if part is None else part + more

        @pl.when(k == 0)
        def _():
            total[...] = part

        @pl.when(k > 0)
        def _():
            total[...] += part

        @pl.when(k == count - 1)
        def _():
            out[...] = total[...].astype(BF)

    return pl.pallas_call(
        kernel,
        grid=(count,),
        out_shape=jax.ShapeDtypeStruct((tok, width), BF),
        in_specs=[pl.BlockSpec((tok, step), lambda k: (0, k))] * len(picks)
        + [pl.BlockSpec((step, width), lambda k: (k, 0))],
        out_specs=pl.BlockSpec((tok, width), lambda k: (0, 0)),
        scratch_shapes=[pltpu.VMEM((tok, width), F32)],
        cost_estimate=pl.CostEstimate(
            flops=300_000_000 * len(picks), bytes_accessed=3_000_000, transcendentals=0
        ),
    )(*picks, rows)


def gate_terms(pick, rows, values):
    slots, tok = pick.shape
    width = rows.shape[1]
    step = slots // CHUNKS
    each = NZ * NX // CHUNKS
    cap = step // each

    def kernel(pick_ref, rows_ref, values_ref, out):
        chosen = jnp.dot(pick_ref[...], values_ref[...], preferred_element_type=F32)
        term = jnp.sum(chosen * rows_ref[...].astype(F32), axis=1, keepdims=True)
        placed = pick_ref[...].astype(F32) * term
        out[...] = jnp.concatenate(
            [
                jnp.sum(placed[n * cap : (n + 1) * cap], axis=0, keepdims=True)
                for n in range(each)
            ],
            axis=0,
        )

    return pl.pallas_call(
        kernel,
        grid=(CHUNKS,),
        out_shape=jax.ShapeDtypeStruct((NZ * NX, tok), F32),
        in_specs=[
            pl.BlockSpec((step, tok), lambda k: (k, 0)),
            pl.BlockSpec((step, width), lambda k: (k, 0)),
            pl.BlockSpec((tok, width), lambda k: (0, 0)),
        ],
        out_specs=pl.BlockSpec((each, tok), lambda k: (k, 0)),
        cost_estimate=pl.CostEstimate(flops=300_000_000, bytes_accessed=3_000_000, transcendentals=0),
        name="gate_terms",
    )(pick, rows, values)


def partial_sums(table, slot_rows, weight, contract):
    slots, width = slot_rows.shape
    rows = slots // (2 * NY)
    hid = weight.shape[1 - contract]
    step = 256

    def kernel(table_ref, weight_ref, rows_ref, keep, away, held, sems):
        @pl.when(pl.program_id(0) == 0)
        def _():
            core = table_ref[4 * NY]
            copies = [
                pltpu.make_async_copy(
                    rows_ref.at[i, h ^ core], held.at[pl.ds((2 * i + h) * rows, rows)], sems.at[i, h]
                )
                for i in range(NY)
                for h in range(2)
            ]
            for c in copies:
                c.start()
            for c in copies:
                c.wait()

        made = lax.dot_general(
            held[...], weight_ref[...], (((1,), (contract,)), ((), ())),
            preferred_element_type=F32,
        )
        for i in range(NY):
            at = i * 2 * rows
            keep[table_ref[i]] = made[at : at + rows]
            away[table_ref[NY + i]] = made[at + rows : at + 2 * rows].astype(BF)

    if contract == 0:
        weight_spec = pl.BlockSpec((width, step), lambda n: (0, n))
    else:
        weight_spec = pl.BlockSpec((step, width), lambda n: (n, 0))
    out_spec = pl.BlockSpec((NY, rows, step), lambda n: (0, 0, n))
    return pl.pallas_call(
        kernel,
        grid=(hid // step,),
        out_shape=[
            jax.ShapeDtypeStruct((NY, rows, hid), F32), jax.ShapeDtypeStruct((NY, rows, hid), BF)
        ],
        in_specs=[SMEM, weight_spec, ANY],
        out_specs=[out_spec] * 2,
        scratch_shapes=[pltpu.VMEM((slots, width), BF), pltpu.SemaphoreType.DMA((NY, 2))],
        cost_estimate=pl.CostEstimate(
            flops=2_400_000_000, bytes_accessed=9_000_000, transcendentals=0
        ),
    )(table, weight, slot_rows.reshape(NY, 2, rows, width))


def expand_rows(table, offset, own, other, weight, contract, made_before=()):
    rows, hid = own.shape[1:]
    width = weight.shape[1 - contract]
    shapes = [
        jax.ShapeDtypeStruct((NY, 2, rows, width), BF),
        jax.ShapeDtypeStruct((NY, 2, rows, hid), BF),
    ]

    def kernel(table_ref, weight_ref, own_ref, other_ref, *refs):
        refs = refs[len(made_before) :]
        out, joined, held, made, held_weight, in_sems, out_sems, join_sems, weight_sem = refs
        core = table_ref[4 * NY]
        fetch = pltpu.make_async_copy(weight_ref, held_weight, weight_sem)
        gets = [
            pltpu.make_async_copy(ref, held.at[n], in_sems.at[n])
            for n, ref in enumerate((own_ref, other_ref))
        ]
        for c in (*gets, fetch):
            c.start()

        def place(n, m):
            return table_ref[offset + NY * n + m], jnp.where(n == 0, core, 1 - core)

        def put(n, m):
            at, half = place(n, m)
            return pltpu.make_async_copy(
                made.at[n, pl.ds(m * rows, rows)], out.at[at, half], out_sems.at[n, m]
            )

        def keep(n, m):
            at, half = place(n, m)
            return pltpu.make_async_copy(held.at[n, m], joined.at[at, half], join_sems.at[n, m])

        fetch.wait()

        def step(n, carry):
            pltpu.make_async_copy(own_ref, held.at[n], in_sems.at[n]).wait()
            for m in range(2):
                keep(n, m).start()
            made[n] = lax.dot_general(
                held[n].reshape(2 * rows, hid), held_weight[...],
                (((1,), (contract,)), ((), ())), preferred_element_type=F32,
            ).astype(BF)
            for m in range(2):
                put(n, m).start()
            return carry

        lax.fori_loop(0, 2, step, 0)
        for n in range(2):
            for m in range(2):
                put(n, m).wait()
                keep(n, m).wait()

    return pl.pallas_call(
        kernel,
        out_shape=shapes,
        in_specs=[SMEM] + [ANY] * (3 + len(made_before)),
        out_specs=[ANY] * 2,
        scratch_shapes=[
            pltpu.VMEM((2, 2, rows, hid), BF),
            pltpu.VMEM((2, 2 * rows, width), BF),
            pltpu.VMEM(weight.shape, BF),
            pltpu.SemaphoreType.DMA((2,)),
            pltpu.SemaphoreType.DMA((2, 2)),
            pltpu.SemaphoreType.DMA((2, 2)),
            pltpu.SemaphoreType.DMA,
        ],
        input_output_aliases={4: 0, 5: 1} if made_before else {},
        cost_estimate=pl.CostEstimate(
            flops=1_200_000_000, bytes_accessed=5_000_000, transcendentals=0
        ),
    )(table, weight, own, other, *made_before)


def weight_grads(left, right, step):
    slots, count = left.shape
    width = right.shape[1]

    def kernel(left_ref, right_ref, out):
        out[...] = lax.dot_general(
            left_ref[...], right_ref[...], (((0,), (0,)), ((), ())), preferred_element_type=F32
        ).astype(BF)

    return pl.pallas_call(
        kernel,
        grid=(count // step,),
        out_shape=jax.ShapeDtypeStruct((count, width), BF),
        in_specs=[
            pl.BlockSpec((slots, step), lambda n: (0, n)),
            pl.BlockSpec((slots, width), lambda n: (0, 0)),
        ],
        out_specs=pl.BlockSpec((step, width), lambda n: (n, 0)),
        cost_estimate=pl.CostEstimate(
            flops=2_400_000_000, bytes_accessed=7_000_000, transcendentals=0
        ),
    )(left, right)


def route_kernel(ids_ref, gates_ref, tokens_ref, pick_ref, hi_ref, lo_ref, rows_ref):
    tok = ids_ref.shape[1]
    each = 8
    cap = pick_ref.shape[0] // each
    chosen, weight = [], []
    for n in range(each):
        hit = jnp.where(ids_ref[...] == pl.program_id(0) * each + n, 1.0, 0.0)
        chosen.append(jnp.sum(hit, axis=0, keepdims=True))
        weight.append(jnp.sum(hit * gates_ref[...], axis=0, keepdims=True))
    chosen = jnp.concatenate(chosen, axis=0)
    earlier = lax.broadcasted_iota(jnp.int32, (tok, tok), 0)
    later = lax.broadcasted_iota(jnp.int32, (tok, tok), 1)
    strict = jnp.where(earlier < later, 1.0, 0.0).astype(BF)
    rank = jnp.dot(chosen.astype(BF), strict, preferred_element_type=F32)
    place = jnp.where(chosen > 0.0, rank, -1.0)
    slot = lax.broadcasted_iota(jnp.int32, (cap, tok), 0).astype(F32)
    one, high, low = [], [], []
    for n in range(each):
        here = slot == place[n : n + 1]
        gate = jnp.where(here, jnp.broadcast_to(weight[n], (cap, tok)), 0.0)
        one.append(jnp.where(here, 1.0, 0.0))
        high.append(gate.astype(BF).astype(F32))
        low.append(gate - high[-1])
    pick = jnp.concatenate(one, axis=0).astype(BF)
    pick_ref[...] = pick
    rows_ref[...] = jnp.dot(pick, tokens_ref[...], preferred_element_type=F32).astype(BF)
    hi_ref[...] = jnp.concatenate(high, axis=0).astype(BF)
    lo_ref[...] = jnp.concatenate(low, axis=0).astype(BF)


def grad_share(keep, got, near, last, pre):
    rows, hid = pre.shape
    step = 16

    def kernel(keep_ref, got_ref, near_ref, last_ref, pre_ref, out):
        def body(n, carry):
            at = pl.ds(pl.multiple_of(n * step, step), step)
            raw = keep_ref[0, at].astype(F32) + got_ref[0, at].astype(F32)
            raw = raw + near_ref[0, at].astype(F32) + last_ref[at].astype(F32)
            pre = pre_ref[at]
            logistic = 1.0 / (1.0 + jnp.exp(-pre))
            out[at] = (raw * (logistic * (1.0 + pre * (1.0 - logistic)))).astype(BF)
            return carry

        lax.fori_loop(0, rows // step, body, 0)

    return pl.pallas_call(
        kernel,
        grid=(1,),
        out_shape=jax.ShapeDtypeStruct((rows, hid), BF),
        in_specs=[
            pl.BlockSpec((1, rows, hid), lambda n: (2, 0, 0)),
            pl.BlockSpec((1, rows, hid), lambda n: (2, 0, 0)),
            pl.BlockSpec((1, rows, hid), lambda n: (0, 0, 0)),
            pl.BlockSpec((rows, hid), lambda n: (0, 0)),
            pl.BlockSpec((rows, hid), lambda n: (0, 0)),
        ],
        out_specs=pl.BlockSpec((rows, hid), lambda n: (0, 0)),
        cost_estimate=pl.CostEstimate(flops=3_000_000, bytes_accessed=3_000_000, transcendentals=200_000),
        name="grad_share",
    )(keep, got, near, last, pre)


def per_device(tokens, cotangent, expert_ids, gates, up_weight, down_weight):
    tok, width = tokens.shape
    top = expert_ids.shape[1]
    experts = NZ * NX
    cap = tok * top * 5 // (4 * experts)
    slots = experts * cap
    y, core = lax.axis_index("y"), lax.axis_index("core")
    w_up, w_down = up_weight[0], down_weight[0]
    hid = w_up.shape[1]

    side_y = 1 - 2 * ((y + core) % 2)
    turn = (jnp.arange(NY, dtype=jnp.int32) - y) % NY

    def share_at(side, places):
        near = jnp.where(turn == side % NY, places[1], places[2])
        return jnp.where(turn == 0, places[0], jnp.where(turn == 2, places[3], near))

    def gathered(side):
        return (y + jnp.stack([0 * side, side, -side, 0 * side + 2])) % NY

    table = jnp.concatenate([
        share_at(side_y, (2, 0, 3, 1)),
        share_at(-side_y, (2, 0, 3, 1)),
        gathered(side_y),
        gathered(-side_y),
        core[None],
    ]).astype(jnp.int32)

    ids_t, gates_t = expert_ids.T, gates.T
    routing = pl.BlockSpec((slots // 4, tok), lambda k: (k, 0))
    small = pl.BlockSpec((top, tok), lambda k: (0, 0))
    pick, gate_hi, gate_lo, x_rows = pl.pallas_call(
        route_kernel,
        grid=(4,),
        out_shape=[jax.ShapeDtypeStruct((slots, tok), BF)] * 3
        + [jax.ShapeDtypeStruct((slots, width), BF)],
        in_specs=[small, small, pl.BlockSpec((tok, width), lambda k: (0, 0))],
        out_specs=[routing] * 3 + [pl.BlockSpec((slots // 4, width), lambda k: (k, 0))],
        name="route",
    )(ids_t, gates_t, tokens)

    def reduce(keep, away):
        got = swap_core(away)
        first = (keep[:2] + got[:2].astype(F32)).astype(BF)
        near = swap(first, 0)
        second = (keep[3] + got[3].astype(F32) + near[1].astype(F32)).astype(BF)
        return got, near, swap(second, 1), first

    def spread(share):
        pair = jnp.stack([share, swap(share, 0)])
        other_pair = swap_core(pair)
        far = swap(pair, 1)
        other_far = swap_core(far)
        return [pair, far, other_pair, other_far]

    x_slots = scatter(x_rows)
    g_slots = scatter(tie(select_rows(pick, (gate_hi, gate_lo), cotangent), x_slots))

    keep, away = partial_sums(table, x_slots, w_up, 0)
    got, near, last, _ = reduce(keep, away)
    pre = keep[2] + got[2].astype(F32) + near[0].astype(F32) + last.astype(F32)
    hidden_shares = spread((pre * jax.nn.sigmoid(pre)).astype(BF))

    keep, away = partial_sums(table, tie(g_slots, hidden_shares[1]), w_down, 1)
    got, near, last, first = reduce(keep, away)
    pair, far, other_pair, other_far = hidden_shares
    begun = expand_rows(table, 2 * NY, pair, other_pair, w_down, 0)
    out_rows, hidden = expand_rows(table, 2 * NY + 2, tie(far, keep), other_far, w_down, 0, begun)
    out_rows, hidden = out_rows.reshape(slots, width), hidden.reshape(slots, hid)
    out_back = scatter(tie(out_rows, first))

    grads = spread(grad_share(keep, got, near, last, pre))
    pair, far, other_pair, other_far = grads
    begun = expand_rows(table, 2 * NY, pair, other_pair, w_up, 1)
    dx_rows, pre_grad = expand_rows(table, 2 * NY + 2, far, other_far, w_up, 1, begun)
    dx_rows, pre_grad = dx_rows.reshape(slots, width), pre_grad.reshape(slots, hid)
    dx_back = scatter(tie(dx_rows, out_back))

    mixed = mix_rows((gate_hi.T, gate_lo.T), out_back)
    terms = gate_terms(pick, tie(out_back, dx_rows), cotangent)
    terms = terms + swap_core(terms)
    terms = terms + swap(terms, 0, False)
    terms = terms + swap(terms, 1, False)
    own = ids_t[:, None, :] == jnp.arange(experts, dtype=jnp.int32)[None, :, None]
    gate_grads = jnp.sum(jnp.where(own, terms[None], 0.0), axis=1).T
    down_grad = weight_grads(tie(hidden, dx_rows), g_slots, 256)
    up_grad = weight_grads(x_slots, pre_grad, 128)
    input_grads = mix_rows((pick.T,), tie(dx_back, down_grad, up_grad, mixed))
    return mixed, input_grads, up_grad[None], down_grad[None], gate_grads


def solution(mesh):
    grid = Mesh(mesh.devices.reshape(NY, 2, NZ, NX), ("y", "core", "z", "x"))
    dp, ex = ("y", "core"), ("z", "x")
    return jax.shard_map(
        per_device,
        mesh=grid,
        in_specs=(P(ex, dp), P(ex, dp), P(ex, None), P(ex, None), P(ex, dp, None), P(ex, None, dp)),
        out_specs=(P(ex, dp), P(ex, dp), P(ex, dp, None), P(ex, None, dp), P(ex, None)),
        check_vma=False,
    )
```

```python
import jax
import jax.numpy as jnp
from jax import lax
from jax.experimental import pallas as pl
from jax.experimental.pallas import tpu as pltpu
from jax.sharding import Mesh
from jax.sharding import PartitionSpec as P

BF = jnp.bfloat16
F32 = jnp.float32

NZ, NX, NY = 8, 4, 4
CHUNKS = 4
FULL = 67_043_328


ANY = pl.BlockSpec(memory_space=pl.ANY)
VMEM = pl.BlockSpec(memory_space=pltpu.VMEM)
SMEM = pl.BlockSpec(memory_space=pltpu.SMEM)


def swap(value, turn, apart=True):
    pairs = []
    for c in range(2):
        for i in range(NY):
            side = 1 if (i + (c if apart else 0) + turn) % 2 == 0 else -1
            pairs.append((2 * i + c, 2 * ((i + side) % NY) + c))
    return lax.ppermute(value, ("y", "core"), pairs)


def swap_core(value):
    return lax.ppermute(value, "core", [(0, 1), (1, 0)])


def tie(value, *others):
    return lax.optimization_barrier((value, *others))[0]


def scatter(rows):
    parts = rows.reshape(NZ * NX, rows.shape[0] // (NZ * NX), rows.shape[1])
    parts = lax.all_to_all(parts, ("z", "x"), split_axis=0, concat_axis=0, tiled=True)
    return parts.reshape(rows.shape)


def select_rows(pick, weights, values):
    slots, tok = pick.shape
    width = values.shape[1]
    step = slots // CHUNKS

    def kernel(pick_ref, *refs):
        weight_refs, (values_ref, out) = refs[: len(weights)], refs[len(weights) :]
        rows = jnp.dot(pick_ref[...], values_ref[...], preferred_element_type=F32)
        if weights:
            rows = rows * sum(
                jnp.sum(w[...].astype(F32), axis=1, keepdims=True) for w in weight_refs
            )
        out[...] = rows.astype(BF)

    chunk = pl.BlockSpec((step, tok), lambda k: (k, 0))
    return pl.pallas_call(
        kernel,
        grid=(CHUNKS,),
        out_shape=jax.ShapeDtypeStruct((slots, width), BF),
        in_specs=[chunk] * (1 + len(weights)) + [pl.BlockSpec((tok, width), lambda k: (0, 0))],
        out_specs=pl.BlockSpec((step, width), lambda k: (k, 0)),
        cost_estimate=pl.CostEstimate(flops=300_000_000, bytes_accessed=3_000_000, transcendentals=0),
        compiler_params=pltpu.CompilerParams(vmem_limit_bytes=FULL),
        name="select_scaled" if weights else "select_plain",
    )(pick, *weights, values)


def mix_rows(picks, rows):
    tok, slots = picks[0].shape
    width = rows.shape[1]
    count = 2
    step = slots // count

    def kernel(*refs):
        pick_refs, (rows_ref, out, total) = refs[: len(picks)], refs[len(picks) :]
        k = pl.program_id(0)
        part = None
        for ref in pick_refs:
            more = jnp.dot(ref[...], rows_ref[...], preferred_element_type=F32)
            part = more if part is None else part + more

        @pl.when(k == 0)
        def _():
            total[...] = part

        @pl.when(k > 0)
        def _():
            total[...] += part

        @pl.when(k == count - 1)
        def _():
            out[...] = total[...].astype(BF)

    return pl.pallas_call(
        kernel,
        grid=(count,),
        out_shape=jax.ShapeDtypeStruct((tok, width), BF),
        in_specs=[pl.BlockSpec((tok, step), lambda k: (0, k))] * len(picks)
        + [pl.BlockSpec((step, width), lambda k: (k, 0))],
        out_specs=pl.BlockSpec((tok, width), lambda k: (0, 0)),
        scratch_shapes=[pltpu.VMEM((tok, width), F32)],
        cost_estimate=pl.CostEstimate(
            flops=300_000_000 * len(picks), bytes_accessed=3_000_000, transcendentals=0
        ),
    )(*picks, rows)


def gate_terms(pick, rows, values):
    slots, tok = pick.shape
    width = rows.shape[1]
    step = slots // CHUNKS
    each = NZ * NX // CHUNKS
    cap = step // each

    def kernel(pick_ref, rows_ref, values_ref, out):
        chosen = jnp.dot(pick_ref[...], values_ref[...], preferred_element_type=F32)
        term = jnp.sum(chosen * rows_ref[...].astype(F32), axis=1, keepdims=True)
        placed = pick_ref[...].astype(F32) * term
        out[...] = jnp.concatenate(
            [
                jnp.sum(placed[n * cap : (n + 1) * cap], axis=0, keepdims=True)
                for n in range(each)
            ],
            axis=0,
        )

    return pl.pallas_call(
        kernel,
        grid=(CHUNKS,),
        out_shape=jax.ShapeDtypeStruct((NZ * NX, tok), F32),
        in_specs=[
            pl.BlockSpec((step, tok), lambda k: (k, 0)),
            pl.BlockSpec((step, width), lambda k: (k, 0)),
            pl.BlockSpec((tok, width), lambda k: (0, 0)),
        ],
        out_specs=pl.BlockSpec((each, tok), lambda k: (k, 0)),
        cost_estimate=pl.CostEstimate(flops=300_000_000, bytes_accessed=3_000_000, transcendentals=0),
        name="gate_terms",
    )(pick, rows, values)


def partial_sums(table, slot_rows, weight, contract):
    slots, width = slot_rows.shape
    rows = slots // (2 * NY)
    hid = weight.shape[1 - contract]
    step = 256

    def kernel(table_ref, weight_ref, rows_ref, keep, away, held, sems):
        @pl.when(pl.program_id(0) == 0)
        def _():
            core = table_ref[4 * NY]
            copies = [
                pltpu.make_async_copy(
                    rows_ref.at[i, h ^ core], held.at[pl.ds((2 * i + h) * rows, rows)], sems.at[i, h]
                )
                for i in range(NY)
                for h in range(2)
            ]
            for c in copies:
                c.start()
            for c in copies:
                c.wait()

        made = lax.dot_general(
            held[...], weight_ref[...], (((1,), (contract,)), ((), ())),
            preferred_element_type=F32,
        )
        for i in range(NY):
            at = i * 2 * rows
            keep[table_ref[i]] = made[at : at + rows]
            away[table_ref[NY + i]] = made[at + rows : at + 2 * rows].astype(BF)

    if contract == 0:
        weight_spec = pl.BlockSpec((width, step), lambda n: (0, n))
    else:
        weight_spec = pl.BlockSpec((step, width), lambda n: (n, 0))
    out_spec = pl.BlockSpec((NY, rows, step), lambda n: (0, 0, n))
    return pl.pallas_call(
        kernel,
        grid=(hid // step,),
        out_shape=[
            jax.ShapeDtypeStruct((NY, rows, hid), F32), jax.ShapeDtypeStruct((NY, rows, hid), BF)
        ],
        in_specs=[SMEM, weight_spec, ANY],
        out_specs=[out_spec] * 2,
        scratch_shapes=[pltpu.VMEM((slots, width), BF), pltpu.SemaphoreType.DMA((NY, 2))],
        cost_estimate=pl.CostEstimate(
            flops=2_400_000_000, bytes_accessed=9_000_000, transcendentals=0
        ),
        compiler_params=pltpu.CompilerParams(vmem_limit_bytes=FULL),
    )(table, weight, slot_rows.reshape(NY, 2, rows, width))


def expand_rows(table, offset, own, other, weight, contract, made_before=()):
    rows, hid = own.shape[1:]
    width = weight.shape[1 - contract]
    shapes = [
        jax.ShapeDtypeStruct((NY, 2, rows, width), BF),
        jax.ShapeDtypeStruct((NY, 2, rows, hid), BF),
    ]

    def kernel(table_ref, weight_ref, own_ref, other_ref, *refs):
        refs = refs[len(made_before) :]
        out, joined, held, made, held_weight, in_sems, out_sems, join_sems, weight_sem = refs
        core = table_ref[4 * NY]
        fetch = pltpu.make_async_copy(weight_ref, held_weight, weight_sem)
        gets = [
            pltpu.make_async_copy(ref, held.at[n], in_sems.at[n])
            for n, ref in enumerate((own_ref, other_ref))
        ]
        for c in (*gets, fetch):
            c.start()

        def place(n, m):
            return table_ref[offset + NY * n + m], jnp.where(n == 0, core, 1 - core)

        def put(n, m):
            at, half = place(n, m)
            return pltpu.make_async_copy(
                made.at[n, pl.ds(m * rows, rows)], out.at[at, half], out_sems.at[n, m]
            )

        def keep(n, m):
            at, half = place(n, m)
            return pltpu.make_async_copy(held.at[n, m], joined.at[at, half], join_sems.at[n, m])

        fetch.wait()

        def step(n, carry):
            pltpu.make_async_copy(own_ref, held.at[n], in_sems.at[n]).wait()
            for m in range(2):
                keep(n, m).start()
            made[n] = lax.dot_general(
                held[n].reshape(2 * rows, hid), held_weight[...],
                (((1,), (contract,)), ((), ())), preferred_element_type=F32,
            ).astype(BF)
            for m in range(2):
                put(n, m).start()
            return carry

        lax.fori_loop(0, 2, step, 0)
        for n in range(2):
            for m in range(2):
                put(n, m).wait()
                keep(n, m).wait()

    return pl.pallas_call(
        kernel,
        out_shape=shapes,
        in_specs=[SMEM] + [ANY] * (3 + len(made_before)),
        out_specs=[ANY] * 2,
        scratch_shapes=[
            pltpu.VMEM((2, 2, rows, hid), BF),
            pltpu.VMEM((2, 2 * rows, width), BF),
            pltpu.VMEM(weight.shape, BF),
            pltpu.SemaphoreType.DMA((2,)),
            pltpu.SemaphoreType.DMA((2, 2)),
            pltpu.SemaphoreType.DMA((2, 2)),
            pltpu.SemaphoreType.DMA,
        ],
        input_output_aliases={4: 0, 5: 1} if made_before else {},
        cost_estimate=pl.CostEstimate(
            flops=1_200_000_000, bytes_accessed=5_000_000, transcendentals=0
        ),
    )(table, weight, own, other, *made_before)


def weight_grads(left, right, step):
    slots, count = left.shape
    width = right.shape[1]

    def kernel(left_ref, right_ref, out):
        out[...] = lax.dot_general(
            left_ref[...], right_ref[...], (((0,), (0,)), ((), ())), preferred_element_type=F32
        ).astype(BF)

    return pl.pallas_call(
        kernel,
        grid=(count // step,),
        out_shape=jax.ShapeDtypeStruct((count, width), BF),
        in_specs=[
            pl.BlockSpec((slots, step), lambda n: (0, n)),
            pl.BlockSpec((slots, width), lambda n: (0, 0)),
        ],
        out_specs=pl.BlockSpec((step, width), lambda n: (n, 0)),
        cost_estimate=pl.CostEstimate(
            flops=2_400_000_000, bytes_accessed=7_000_000, transcendentals=0
        ),
        compiler_params=pltpu.CompilerParams(vmem_limit_bytes=FULL),
    )(left, right)


def route_kernel(ids_ref, gates_ref, tokens_ref, pick_ref, hi_ref, lo_ref, rows_ref):
    tok = ids_ref.shape[1]
    each = 8
    cap = pick_ref.shape[0] // each
    chosen, weight = [], []
    for n in range(each):
        hit = jnp.where(ids_ref[...] == pl.program_id(0) * each + n, 1.0, 0.0)
        chosen.append(jnp.sum(hit, axis=0, keepdims=True))
        weight.append(jnp.sum(hit * gates_ref[...], axis=0, keepdims=True))
    chosen = jnp.concatenate(chosen, axis=0)
    earlier = lax.broadcasted_iota(jnp.int32, (tok, tok), 0)
    later = lax.broadcasted_iota(jnp.int32, (tok, tok), 1)
    strict = jnp.where(earlier < later, 1.0, 0.0).astype(BF)
    rank = jnp.dot(chosen.astype(BF), strict, preferred_element_type=F32)
    place = jnp.where(chosen > 0.0, rank, -1.0)
    slot = lax.broadcasted_iota(jnp.int32, (cap, tok), 0).astype(F32)
    one, high, low = [], [], []
    for n in range(each):
        here = slot == place[n : n + 1]
        gate = jnp.where(here, jnp.broadcast_to(weight[n], (cap, tok)), 0.0)
        one.append(jnp.where(here, 1.0, 0.0))
        high.append(gate.astype(BF).astype(F32))
        low.append(gate - high[-1])
    pick = jnp.concatenate(one, axis=0).astype(BF)
    pick_ref[...] = pick
    rows_ref[...] = jnp.dot(pick, tokens_ref[...], preferred_element_type=F32).astype(BF)
    hi_ref[...] = jnp.concatenate(high, axis=0).astype(BF)
    lo_ref[...] = jnp.concatenate(low, axis=0).astype(BF)


def grad_share(keep, got, near, last, pre):
    rows, hid = pre.shape
    step = 16

    def kernel(keep_ref, got_ref, near_ref, last_ref, pre_ref, out):
        def body(n, carry):
            at = pl.ds(pl.multiple_of(n * step, step), step)
            raw = keep_ref[0, at].astype(F32) + got_ref[0, at].astype(F32)
            raw = raw + near_ref[0, at].astype(F32) + last_ref[at].astype(F32)
            pre = pre_ref[at]
            logistic = 1.0 / (1.0 + jnp.exp(-pre))
            out[at] = (raw * (logistic * (1.0 + pre * (1.0 - logistic)))).astype(BF)
            return carry

        lax.fori_loop(0, rows // step, body, 0)

    return pl.pallas_call(
        kernel,
        grid=(1,),
        out_shape=jax.ShapeDtypeStruct((rows, hid), BF),
        in_specs=[
            pl.BlockSpec((1, rows, hid), lambda n: (2, 0, 0)),
            pl.BlockSpec((1, rows, hid), lambda n: (2, 0, 0)),
            pl.BlockSpec((1, rows, hid), lambda n: (0, 0, 0)),
            pl.BlockSpec((rows, hid), lambda n: (0, 0)),
            pl.BlockSpec((rows, hid), lambda n: (0, 0)),
        ],
        out_specs=pl.BlockSpec((rows, hid), lambda n: (0, 0)),
        cost_estimate=pl.CostEstimate(flops=3_000_000, bytes_accessed=3_000_000, transcendentals=200_000),
        compiler_params=pltpu.CompilerParams(vmem_limit_bytes=FULL),
        name="grad_share",
    )(keep, got, near, last, pre)


def per_device(tokens, cotangent, expert_ids, gates, up_weight, down_weight):
    tok, width = tokens.shape
    top = expert_ids.shape[1]
    experts = NZ * NX
    cap = tok * top * 5 // (4 * experts)
    slots = experts * cap
    y, core = lax.axis_index("y"), lax.axis_index("core")
    w_up, w_down = up_weight[0], down_weight[0]
    hid = w_up.shape[1]

    side_y = 1 - 2 * ((y + core) % 2)
    turn = (jnp.arange(NY, dtype=jnp.int32) - y) % NY

    def share_at(side, places):
        near = jnp.where(turn == side % NY, places[1], places[2])
        return jnp.where(turn == 0, places[0], jnp.where(turn == 2, places[3], near))

    def gathered(side):
        return (y + jnp.stack([0 * side, side, -side, 0 * side + 2])) % NY

    table = jnp.concatenate([
        share_at(side_y, (2, 0, 3, 1)),
        share_at(-side_y, (2, 0, 3, 1)),
        gathered(side_y),
        gathered(-side_y),
        core[None],
    ]).astype(jnp.int32)

    ids_t, gates_t = expert_ids.T, gates.T
    routing = pl.BlockSpec((slots // 4, tok), lambda k: (k, 0))
    small = pl.BlockSpec((top, tok), lambda k: (0, 0))
    pick, gate_hi, gate_lo, x_rows = pl.pallas_call(
        route_kernel,
        grid=(4,),
        out_shape=[jax.ShapeDtypeStruct((slots, tok), BF)] * 3
        + [jax.ShapeDtypeStruct((slots, width), BF)],
        in_specs=[small, small, pl.BlockSpec((tok, width), lambda k: (0, 0))],
        out_specs=[routing] * 3 + [pl.BlockSpec((slots // 4, width), lambda k: (k, 0))],
        name="route",
    )(ids_t, gates_t, tokens)

    def reduce(keep, away):
        got = swap_core(away)
        first = (keep[:2] + got[:2].astype(F32)).astype(BF)
        near = swap(first, 0)
        second = (keep[3] + got[3].astype(F32) + near[1].astype(F32)).astype(BF)
        return got, near, swap(second, 1), first

    def spread(share):
        pair = jnp.stack([share, swap(share, 0)])
        other_pair = swap_core(pair)
        far = swap(pair, 1)
        other_far = swap_core(far)
        return [pair, far, other_pair, other_far]

    x_slots = scatter(x_rows)
    g_slots = scatter(tie(select_rows(pick, (gate_hi, gate_lo), cotangent), x_slots))

    keep, away = partial_sums(table, x_slots, w_up, 0)
    got, near, last, _ = reduce(keep, away)
    pre = keep[2] + got[2].astype(F32) + near[0].astype(F32) + last.astype(F32)
    hidden_shares = spread((pre * jax.nn.sigmoid(pre)).astype(BF))

    keep, away = partial_sums(table, tie(g_slots, hidden_shares[1]), w_down, 1)
    got, near, last, first = reduce(keep, away)
    pair, far, other_pair, other_far = hidden_shares
    begun = expand_rows(table, 2 * NY, pair, other_pair, w_down, 0)
    out_rows, hidden = expand_rows(table, 2 * NY + 2, tie(far, keep), other_far, w_down, 0, begun)
    out_rows, hidden = out_rows.reshape(slots, width), hidden.reshape(slots, hid)
    out_back = scatter(tie(out_rows, first))

    grads = spread(grad_share(keep, got, near, last, pre))
    pair, far, other_pair, other_far = grads
    begun = expand_rows(table, 2 * NY, pair, other_pair, w_up, 1)
    dx_rows, pre_grad = expand_rows(table, 2 * NY + 2, far, other_far, w_up, 1, begun)
    dx_rows, pre_grad = dx_rows.reshape(slots, width), pre_grad.reshape(slots, hid)
    dx_back = scatter(tie(dx_rows, out_back))

    mixed = mix_rows((gate_hi.T, gate_lo.T), out_back)
    terms = gate_terms(pick, tie(out_back, dx_rows), cotangent)
    terms = terms + swap_core(terms)
    terms = terms + swap(terms, 0, False)
    terms = terms + swap(terms, 1, False)
    own = ids_t[:, None, :] == jnp.arange(experts, dtype=jnp.int32)[None, :, None]
    gate_grads = jnp.sum(jnp.where(own, terms[None], 0.0), axis=1).T
    down_grad = weight_grads(tie(hidden, dx_rows), g_slots, 256)
    up_grad = weight_grads(x_slots, pre_grad, 128)
    input_grads = mix_rows((pick.T,), tie(dx_back, down_grad, up_grad, mixed))
    return mixed, input_grads, up_grad[None], down_grad[None], gate_grads


def solution(mesh):
    grid = Mesh(mesh.devices.reshape(NY, 2, NZ, NX), ("y", "core", "z", "x"))
    dp, ex = ("y", "core"), ("z", "x")
    return jax.shard_map(
        per_device,
        mesh=grid,
        in_specs=(P(ex, dp), P(ex, dp), P(ex, None), P(ex, None), P(ex, dp, None), P(ex, None, dp)),
        out_specs=(P(ex, dp), P(ex, dp), P(ex, dp, None), P(ex, None, dp), P(ex, None)),
        check_vma=False,
    )
```
